32 devices in a mesh: groups: 2 (over y), ens: 4 (over z), amp: 4 (over x, core).
Axes of the slice: x: 2, y: 2, z: 4, core: 2. Of those that a mesh axis runs over, the one named last changes fastest.
Arguments:
- states: bfloat16 [64, 2, 262144], P(('groups', 'ens'), None, 'amp'), parts along dimension 0, may hold values from -6 to 6
- layer_angles: int32 [64, 16, 7, 2], P(('groups', 'ens')), parts along dimension 0, may hold values from 0 to 63
- entangler: int32 [64, 16, 6], P(('groups', 'ens')), parts along dimension 0, may hold values 0 or 1
- global_angles: int32 [64, 2], P(('groups', 'ens')), parts along dimension 0, may hold values from 0 to 63
Outputs:
- correlations: float32 [2, 64, 32], P(None, ('groups', 'ens'), 'amp'), parts along dimension 1
The draws below stay inside these ranges and needn't reach their ends.
There are 2 independent parts, one for each index of `groups`. The reference program is written for one: setup_inputs(seed, part) draws one part's arguments, and reference() takes and returns one part's arrays. A program takes and returns all parts, laid end to end along the dimension named above; each array names one. Nothing has to cross between parts.
All inputs are finite; a program needn't handle non-finite values. No bound on the sum of `entangler` on one device may be relied on, other than what follows from the above.
Results may differ from the reference program's by a relative error of at most 0.035.
Values may be sent and summed in bfloat16 or wider, within the bound.
A program may use at most 64 MiB of HBM per device.

```python
import math
import jax
import jax.numpy as jnp
from jax import lax

JOINED = 7
LAYERS = 16
TABLE = 64
CIRC = 32
AMPS = 262144


def place_ends(entries, rng, smallest, high):
    shape = entries.shape
    place = [jax.random.randint(jax.random.fold_in(rng, axis), (), 0, shape[axis]) for axis in range(len(shape))]
    entries = entries.at[tuple(place)].set(smallest)
    longest = shape.index(max(shape))
    place[longest] = (place[longest] + 1) % shape[longest]
    return entries.at[tuple(place)].set(high)


def steps_of(rng, shape, shards, least, top_value):
    factor_of = 1.0
    for position, parts in shards:
        heights = jax.random.uniform(jax.random.fold_in(jax.random.fold_in(rng, 6), position), (parts,), jnp.float32, least / len(shards), top_value / len(shards))
        factor_of = factor_of * jnp.repeat(jnp.exp(heights), shape[position] // parts).reshape((-1,) + (1,) * (len(shape) - 1 - position))
    return factor_of


def noise(stream_key, extent, spread, reach, shards=(), kind=jnp.bfloat16):
    values = jax.random.normal(stream_key, extent, jnp.float32) * spread
    if len(shards) > 0:
        values = steps_of(stream_key, extent, shards, -0.22, 0.18) * values
    return jnp.clip(values, min=-reach, max=reach).astype(kind)


def setup_inputs(seed: int = 0, part: int = 0) -> dict:
    seeds = jax.random.split(jax.random.key(seed), 5)
    part_splits = jax.random.split(jax.random.fold_in(seeds[4], part), 5)
    return {
        "states": noise(part_splits[0], (CIRC, 2, AMPS), 1.0, 6.0, ((0, 4), (2, 4))),
        "layer_angles": place_ends(jax.random.randint(part_splits[1], (CIRC, LAYERS, JOINED, 2), 0, TABLE), jax.random.fold_in(part_splits[1], 1), 0, TABLE - 1).astype(jnp.int32),
        "entangler": place_ends((jax.random.randint(part_splits[2], (CIRC, LAYERS, JOINED - 1), 0, 2) < 1).astype(jnp.int32), jax.random.fold_in(part_splits[2], 1), 0, 1),
        "global_angles": place_ends(jax.random.randint(part_splits[3], (CIRC, 2), 0, TABLE), jax.random.fold_in(part_splits[3], 1), 0, TABLE - 1).astype(jnp.int32),
    }


def rotation(polar_index, azimuth_index):
    polar = polar_index.astype(jnp.float32) * (math.pi / TABLE)
    azimuth = azimuth_index.astype(jnp.float32) * (math.pi / TABLE)
    cos_polar = jnp.cos(polar)
    sin_polar = jnp.sin(polar)
    cos_azim = jnp.cos(azimuth)
    sin_azim = jnp.sin(azimuth)
    return ((cos_azim * cos_polar, -sin_azim * cos_polar), (-cos_azim * sin_polar, sin_azim * sin_polar), (cos_azim * sin_polar, sin_azim * sin_polar), (cos_azim * cos_polar, sin_azim * cos_polar))

def pick_entry(gate, which, out_bit, in_bit):
    first = gate[0][which][:, None, None]
    second = gate[1][which][:, None, None]
    third = gate[2][which][:, None, None]
    fourth = gate[3][which][:, None, None]
    return jnp.where(out_bit == 0, jnp.where(in_bit == 0, first, second), jnp.where(in_bit == 0, third, fourth))

def layer_weights(angles, links):
    order = 2 ** JOINED
    circuits = angles.shape[0]
    index_row = jnp.arange(order, dtype=jnp.int32)
    real_part = jnp.ones((circuits, order, order), jnp.float32)
    imag_part = jnp.zeros((circuits, order, order), jnp.float32)
    for qubit_index in range(JOINED):
        gate = rotation(angles[:, qubit_index, 0], angles[:, qubit_index, 1])
        bit_row = index_row // 2 ** qubit_index % 2
        out_bit = bit_row[None, :, None]
        in_bit = bit_row[None, None, :]
        factor_real = pick_entry(gate, 0, out_bit, in_bit)
        factor_imag = pick_entry(gate, 1, out_bit, in_bit)
        real_part, imag_part = (real_part * factor_real - imag_part * factor_imag, real_part * factor_imag + imag_part * factor_real)
    sign_flip = jnp.ones((circuits, order), jnp.float32)
    for qubit_index in range(JOINED - 1):
        both_set = index_row // 2 ** qubit_index % 2 * (index_row // 2 ** (qubit_index + 1) % 2)
        flipped = links[:, qubit_index][:, None] * both_set[None, :]
        sign_flip = sign_flip * (1.0 - 2.0 * flipped.astype(jnp.float32))
    real_part = real_part * sign_flip[:, :, None]
    imag_part = imag_part * sign_flip[:, :, None]
    real_turned = jnp.transpose(real_part, (0, 2, 1))
    imag_turned = jnp.transpose(imag_part, (0, 2, 1))
    top_row = jnp.stack([real_turned, imag_turned], 1)
    bottom_row = jnp.stack([-imag_turned, real_turned], 1)
    return jnp.stack([top_row, bottom_row], 1).astype(jnp.bfloat16)

def bridge_signs(local):
    index_all = jnp.arange(local, dtype=jnp.int32)
    both_set = index_all // 2 ** (JOINED - 1) % 2 * (index_all // 2 ** JOINED % 2)
    return 1.0 - 2.0 * both_set.astype(jnp.float32)

def apply_layer(current, weights, upper_block):
    circuits, _, local = current.shape
    order = weights.shape[-1]
    matrices = weights.astype(jnp.float32)
    if upper_block:
        reshaped = current.astype(jnp.float32).reshape(circuits, 2, local // (order * order), order, order)
        result = jnp.einsum('cphnl,cpqnm->cqhml', reshaped, matrices, precision=lax.Precision.HIGHEST)
    else:
        reshaped = current.astype(jnp.float32).reshape(circuits, 2, local // order, order)
        result = jnp.einsum('cprn,cpqnm->cqrm', reshaped, matrices, precision=lax.Precision.HIGHEST)
    result = result.reshape(circuits, 2, local) * bridge_signs(local)[None, None, :]
    return result.astype(jnp.bfloat16)

def scaled(coefficient, amplitudes):
    real_c = coefficient[0][:, None]
    imag_c = coefficient[1][:, None]
    return jnp.stack([real_c * amplitudes[:, 0] - imag_c * amplitudes[:, 1], real_c * amplitudes[:, 1] + imag_c * amplitudes[:, 0]], 1)

def reference(states, layer_angles, entangler, global_angles):
    current = states
    for layer in range(LAYERS):
        weights = layer_weights(layer_angles[:, layer], entangler[:, layer])
        current = apply_layer(current, weights, layer % 2 == 1)
    halfway = AMPS // 2
    lower_amps = current[:, :, :halfway].astype(jnp.float32)
    upper_amps = current[:, :, halfway:].astype(jnp.float32)
    gate = rotation(global_angles[:, 0], global_angles[:, 1])
    new_lower = scaled(gate[0], lower_amps) + scaled(gate[1], upper_amps)
    new_upper = scaled(gate[2], lower_amps) + scaled(gate[3], upper_amps)
    final_states = jnp.concatenate([new_lower, new_upper], 2).astype(jnp.bfloat16)
    real_amps = final_states[:, 0]
    imag_amps = final_states[:, 1]
    gram_real = jnp.dot(real_amps, real_amps.T, preferred_element_type=jnp.float32) + jnp.dot(imag_amps, imag_amps.T, preferred_element_type=jnp.float32)
    gram_imag = jnp.dot(real_amps, imag_amps.T, preferred_element_type=jnp.float32) - jnp.dot(imag_amps, real_amps.T, preferred_element_type=jnp.float32)
    circuit_row = jnp.arange(CIRC, dtype=jnp.int32)
    off_diagonal = jnp.where(circuit_row[:, None] == circuit_row[None, :], 0.0, 1.0).astype(jnp.float32)
    factor = off_diagonal / math.sqrt(AMPS)
    return jnp.stack([gram_real * factor, gram_imag * factor])
```

```python
import functools
import math

import jax
import jax.numpy as jnp
from jax import lax
from jax.experimental import pallas as pl
from jax.experimental.pallas import tpu as pltpu
from jax.sharding import PartitionSpec as P

JOINED = 7
TABLE = 64
ORDER = 2**JOINED
LOW = 3
GROUP = 2


def from_partner(array, axis, bit):
    return lax.ppermute(array, axis, [(i, i ^ 1 << bit) for i in range(lax.axis_size(axis))])


def rotation(polar_index, azimuth_index):
    polar = polar_index.astype(jnp.float32) * (math.pi / TABLE)
    azimuth = azimuth_index.astype(jnp.float32) * (math.pi / TABLE)
    cos_polar = jnp.cos(polar)
    sin_polar = jnp.sin(polar)
    cos_azim = jnp.cos(azimuth)
    sin_azim = jnp.sin(azimuth)
    return (
        (cos_azim * cos_polar, -sin_azim * cos_polar),
        (-cos_azim * sin_polar, sin_azim * sin_polar),
        (cos_azim * sin_polar, sin_azim * sin_polar),
        (cos_azim * cos_polar, sin_azim * cos_polar),
    )


def bit_of(shape, dim, bit, shift=0):
    return (lax.broadcasted_iota(jnp.int32, shape, dim) >> (bit - shift)) & 1


def part_factor(cos_ref, sin_ref, flip_ref, at, upper, high):
    qubits = range(LOW, JOINED) if high else range(LOW)
    shape = (2 ** len(qubits), ORDER)
    shift = LOW if high else 0
    row = {k: bit_of(shape, 0, k, shift) for k in qubits}
    lane = {k: bit_of(shape, 1, k) for k in range(JOINED)}
    out = row if upper else lane
    real = imag = None
    turn = None
    for k in qubits:
        cos_t, sin_t = cos_ref[at * 14 + 2 * k], sin_ref[at * 14 + 2 * k]
        cos_f, sin_f = cos_ref[at * 14 + 2 * k + 1], sin_ref[at * 14 + 2 * k + 1]
        side = (2 * out[k] - 1).astype(jnp.float32)
        factor = jnp.where(row[k] == lane[k], cos_t, side * sin_t)
        turn = factor if turn is None else turn * factor
        step = side * sin_f
        if real is None:
            real, imag = jnp.full(shape, cos_f), step
        else:
            real, imag = real * cos_f - imag * step, real * step + imag * cos_f
    for k in range(JOINED - 1):
        inside = k in qubits and k + 1 in qubits
        if inside or (not upper and not high and k == LOW - 1):
            turn = jnp.where(out[k] * out[k + 1] == 1, flip_ref[at * 6 + k] * turn, turn)
    return real * turn, imag * turn


def build(cos_ref, sin_ref, flip_ref, at, upper, w_ref):
    low_real, low_imag = part_factor(cos_ref, sin_ref, flip_ref, at, upper, False)
    high_real, high_imag = part_factor(cos_ref, sin_ref, flip_ref, at, upper, True)
    lows = [(low_real, low_imag)] * 2
    if upper:
        crossed = bit_of(low_real.shape, 0, LOW - 1) == 1
        flip = flip_ref[at * 6 + LOW - 1]
        lows[1] = tuple(jnp.where(crossed, flip * v, v) for v in lows[0])
    for pair in range(ORDER // 16):
        reals, imags = [], []
        for odd in range(2):
            r = 2 * pair + odd
            a_real = jnp.broadcast_to(high_real[r : r + 1], (8, ORDER))
            a_imag = jnp.broadcast_to(high_imag[r : r + 1], (8, ORDER))
            b_real, b_imag = lows[odd]
            reals.append(a_real * b_real - a_imag * b_imag)
            imags.append(a_real * b_imag + a_imag * b_real)
        real = jnp.concatenate(reals, 0)
        imag = jnp.concatenate(imags, 0)
        plus, minus = imag.astype(jnp.bfloat16), (-imag).astype(jnp.bfloat16)
        real = real.astype(jnp.bfloat16)
        top, bottom = (minus, plus) if upper else (plus, minus)
        rows = pl.ds(16 * pair, 16)
        rows_below = pl.ds(ORDER + 16 * pair, 16)
        w_ref[rows, :ORDER] = real
        w_ref[rows, ORDER:] = top
        w_ref[rows_below, :ORDER] = bottom
        w_ref[rows_below, ORDER:] = real


def bridge(values):
    rows, columns = values.shape
    shape = (1, 8, columns)
    odd = bit_of(shape, 1, 0) * bit_of(shape, 2, JOINED - 1)
    sign = (1 - 2 * odd).astype(jnp.float32)
    return (values.reshape(rows // 8, 8, columns) * sign).reshape(rows, columns)


def run_layers(first, layers, cos_ref, sin_ref, flip_ref, x_refs, t_refs, wl_ref, wu_ref, s_ref):
    rows = t_refs[0].shape[0]
    blocks = rows // ORDER
    many = len(t_refs)
    for i in range(many):
        t_refs[i][:, :ORDER] = x_refs[i][0]
        t_refs[i][:, ORDER:] = x_refs[i][1]
        build(cos_ref, sin_ref, flip_ref, (first + i) * layers, False, wl_ref.at[i])

    def two(pair, carry):
        layer = 2 * pair
        following = jnp.minimum(layer + 2, layers - 2)
        for i in range(many):
            at = (first + i) * layers
            y = jnp.dot(t_refs[i][...], wl_ref[i], preferred_element_type=jnp.float32)
            y = bridge(y).astype(jnp.bfloat16)
            for b in range(blocks):
                for p in range(2):
                    s_ref[i, p * ORDER : (p + 1) * ORDER, b * ORDER : (b + 1) * ORDER] = y[
                        b * ORDER : (b + 1) * ORDER, p * ORDER : (p + 1) * ORDER
                    ]
            build(cos_ref, sin_ref, flip_ref, at + layer + 1, True, wu_ref.at[i])
        for i in range(many):
            at = (first + i) * layers
            y = jnp.dot(wu_ref[i], s_ref[i], preferred_element_type=jnp.float32)
            y = bridge(y).astype(jnp.bfloat16)
            for b in range(blocks):
                for p in range(2):
                    t_refs[i][b * ORDER : (b + 1) * ORDER, p * ORDER : (p + 1) * ORDER] = y[
                        p * ORDER : (p + 1) * ORDER, b * ORDER : (b + 1) * ORDER
                    ]
            build(cos_ref, sin_ref, flip_ref, at + following, False, wl_ref.at[i])
        return carry

    lax.fori_loop(0, layers // 2, two, 0)


def layers_scratch(rows):
    return [
        pltpu.VMEM((GROUP, 2 * ORDER, 2 * ORDER), jnp.bfloat16),
        pltpu.VMEM((GROUP, 2 * ORDER, 2 * ORDER), jnp.bfloat16),
        pltpu.VMEM((GROUP, 2 * ORDER, rows), jnp.bfloat16),
    ]


def layers_kernel(layers, cos_ref, sin_ref, flip_ref, x_ref, t_ref, wl_ref, wu_ref, s_ref):
    first = pl.program_id(0) * GROUP
    run_layers(
        first, layers, cos_ref, sin_ref, flip_ref,
        [x_ref.at[i] for i in range(GROUP)], [t_ref.at[i] for i in range(GROUP)],
        wl_ref, wu_ref, s_ref,
    )


def small_tables(layer_angles, entangler):
    angle = layer_angles.astype(jnp.float32).reshape(-1) * (math.pi / TABLE)
    flip = 1.0 - 2.0 * entangler.astype(jnp.float32).reshape(-1)
    return jnp.cos(angle), jnp.sin(angle), flip


def all_layers(states, layer_angles, entangler):
    circuits, _, local = states.shape
    rows = local // ORDER
    layers = layer_angles.shape[1]
    smem = pl.BlockSpec(memory_space=pltpu.SMEM)
    return pl.pallas_call(
        functools.partial(layers_kernel, layers),
        grid=(circuits // GROUP,),
        out_shape=jax.ShapeDtypeStruct((circuits, rows, 2 * ORDER), jnp.bfloat16),
        in_specs=[smem, smem, smem, pl.BlockSpec((GROUP, 2, rows, ORDER), lambda g: (g, 0, 0, 0))],
        out_specs=pl.BlockSpec((GROUP, rows, 2 * ORDER), lambda g: (g, 0, 0)),
        scratch_shapes=layers_scratch(rows),
        compiler_params=pltpu.CompilerParams(vmem_limit_bytes=32 << 20),
    )(*small_tables(layer_angles, entangler), states.reshape(circuits, 2, rows, ORDER))


def scaled(coefficient, amplitudes):
    real_c = coefficient[0][:, None]
    imag_c = coefficient[1][:, None]
    return jnp.stack(
        [
            real_c * amplitudes[:, 0] - imag_c * amplitudes[:, 1],
            real_c * amplitudes[:, 1] + imag_c * amplitudes[:, 0],
        ],
        1,
    )


def choose_pair(upper_side, when_lower, when_upper):
    return (
        jnp.where(upper_side == 0, when_lower[0], when_upper[0]),
        jnp.where(upper_side == 0, when_lower[1], when_upper[1]),
    )


def pair_tile(mine, remote):
    products = jnp.einsum("ipa,jqa->pqij", mine, remote, preferred_element_type=jnp.float32)
    return jnp.stack([products[0, 0] + products[1, 1], products[0, 1] - products[1, 0]])


def body(states, layer_angles, entangler, global_angles):
    circuits = states.shape[0]

    turned = all_layers(states, layer_angles, entangler).reshape(circuits, -1, 2, ORDER)
    current = jnp.swapaxes(turned, 1, 2).reshape(states.shape)
    swap_bit = lax.axis_size("amp").bit_length() - 2
    upper_side = lax.axis_index("amp") // 2**swap_bit % 2
    gate = rotation(global_angles[:, 0], global_angles[:, 1])
    partner = from_partner(current, "amp", swap_bit)
    coeff_self = choose_pair(upper_side, gate[0], gate[3])
    coeff_other = choose_pair(upper_side, gate[1], gate[2])
    final_states = (
        scaled(coeff_self, current.astype(jnp.float32))
        + scaled(coeff_other, partner.astype(jnp.float32))
    ).astype(jnp.bfloat16)
    own_block = lax.axis_index("ens")
    partials = pair_tile(final_states, lax.all_gather(final_states, "ens", axis=0, tiled=True))
    summed = lax.psum_scatter(partials, "amp", scatter_dimension=2, tiled=True)
    columns = summed.shape[2]
    row_index = own_block * circuits + jnp.arange(circuits, dtype=jnp.int32)
    column_index = lax.axis_index("amp") * columns + jnp.arange(columns, dtype=jnp.int32)
    off_diagonal = jnp.where(row_index[:, None] == column_index[None, :], 0.0, 1.0).astype(
        jnp.float32
    )
    amplitudes = states.shape[2] * lax.axis_size("amp")
    return summed * (off_diagonal / math.sqrt(amplitudes))[None]


def solution(mesh):
    return jax.shard_map(
        body,
        mesh=mesh,
        in_specs=(
            P(("groups", "ens"), None, "amp"),
            P(("groups", "ens"), None, None, None),
            P(("groups", "ens"), None, None),
            P(("groups", "ens"), None),
        ),
        out_specs=P(None, ("groups", "ens"), "amp"),
        check_vma=False,
    )
```

```python
import functools
import math

import jax
import jax.numpy as jnp
from jax import lax
from jax.experimental import pallas as pl
from jax.experimental.pallas import tpu as pltpu
from jax.sharding import PartitionSpec as P

JOINED = 7
TABLE = 64
ORDER = 2**JOINED
LOW = 3
GROUP = 2


def from_partner(array, axis, bit):
    return lax.ppermute(array, axis, [(i, i ^ 1 << bit) for i in range(lax.axis_size(axis))])


def rotation(polar_index, azimuth_index):
    polar = polar_index.astype(jnp.float32) * (math.pi / TABLE)
    azimuth = azimuth_index.astype(jnp.float32) * (math.pi / TABLE)
    cos_polar = jnp.cos(polar)
    sin_polar = jnp.sin(polar)
    cos_azim = jnp.cos(azimuth)
    sin_azim = jnp.sin(azimuth)
    return (
        (cos_azim * cos_polar, -sin_azim * cos_polar),
        (-cos_azim * sin_polar, sin_azim * sin_polar),
        (cos_azim * sin_polar, sin_azim * sin_polar),
        (cos_azim * cos_polar, sin_azim * cos_polar),
    )


def bit_of(shape, dim, bit, shift=0):
    return (lax.broadcasted_iota(jnp.int32, shape, dim) >> (bit - shift)) & 1


def part_factor(cos_ref, sin_ref, flip_ref, at, upper, high):
    qubits = range(LOW, JOINED) if high else range(LOW)
    shape = (2 ** len(qubits), ORDER)
    shift = LOW if high else 0
    row = {k: bit_of(shape, 0, k, shift) for k in qubits}
    lane = {k: bit_of(shape, 1, k) for k in range(JOINED)}
    out = row if upper else lane
    real = imag = None
    turn = None
    for k in qubits:
        cos_t, sin_t = cos_ref[at * 14 + 2 * k], sin_ref[at * 14 + 2 * k]
        cos_f, sin_f = cos_ref[at * 14 + 2 * k + 1], sin_ref[at * 14 + 2 * k + 1]
        side = (2 * out[k] - 1).astype(jnp.float32)
        factor = jnp.where(row[k] == lane[k], cos_t, side * sin_t)
        turn = factor if turn is None else turn * factor
        step = side * sin_f
        if real is None:
            real, imag = jnp.full(shape, cos_f), step
        else:
            real, imag = real * cos_f - imag * step, real * step + imag * cos_f
    for k in range(JOINED - 1):
        inside = k in qubits and k + 1 in qubits
        if inside or (not upper and not high and k == LOW - 1):
            turn = jnp.where(out[k] * out[k + 1] == 1, flip_ref[at * 6 + k] * turn, turn)
    return real * turn, imag * turn


def build(cos_ref, sin_ref, flip_ref, at, upper, w_ref):
    low_real, low_imag = part_factor(cos_ref, sin_ref, flip_ref, at, upper, False)
    high_real, high_imag = part_factor(cos_ref, sin_ref, flip_ref, at, upper, True)
    lows = [(low_real, low_imag)] * 2
    if upper:
        crossed = bit_of(low_real.shape, 0, LOW - 1) == 1
        flip = flip_ref[at * 6 + LOW - 1]
        lows[1] = tuple(jnp.where(crossed, flip * v, v) for v in lows[0])
    for pair in range(ORDER // 16):
        reals, imags = [], []
        for odd in range(2):
            r = 2 * pair + odd
            a_real = jnp.broadcast_to(high_real[r : r + 1], (8, ORDER))
            a_imag = jnp.broadcast_to(high_imag[r : r + 1], (8, ORDER))
            b_real, b_imag = lows[odd]
            reals.append(a_real * b_real - a_imag * b_imag)
            imags.append(a_real * b_imag + a_imag * b_real)
        real = jnp.concatenate(reals, 0)
        imag = jnp.concatenate(imags, 0)
        plus, minus = imag.astype(jnp.bfloat16), (-imag).astype(jnp.bfloat16)
        real = real.astype(jnp.bfloat16)
        top, bottom = (minus, plus) if upper else (plus, minus)
        rows = pl.ds(16 * pair, 16)
        rows_below = pl.ds(ORDER + 16 * pair, 16)
        w_ref[rows, :ORDER] = real
        w_ref[rows, ORDER:] = top
        w_ref[rows_below, :ORDER] = bottom
        w_ref[rows_below, ORDER:] = real


def bridge(values):
    rows, columns = values.shape
    shape = (1, 8, columns)
    odd = bit_of(shape, 1, 0) * bit_of(shape, 2, JOINED - 1)
    sign = (1 - 2 * odd).astype(jnp.float32)
    return (values.reshape(rows // 8, 8, columns) * sign).reshape(rows, columns)


def run_layers(first, layers, cos_ref, sin_ref, flip_ref, x_refs, t_refs, wl_ref, wu_ref, s_ref):
    rows = t_refs[0].shape[0]
    blocks = rows // ORDER
    many = len(t_refs)
    for i in range(many):
        t_refs[i][:, :ORDER] = x_refs[i][0]
        t_refs[i][:, ORDER:] = x_refs[i][1]
        build(cos_ref, sin_ref, flip_ref, (first + i) * layers, False, wl_ref.at[i])

    def two(pair, carry):
        layer = 2 * pair
        following = jnp.minimum(layer + 2, layers - 2)
        for i in range(many):
            at = (first + i) * layers
            y = jnp.dot(t_refs[i][...], wl_ref[i], preferred_element_type=jnp.float32)
            y = bridge(y).astype(jnp.bfloat16)
            for b in range(blocks):
                for p in range(2):
                    s_ref[i, p * ORDER : (p + 1) * ORDER, b * ORDER : (b + 1) * ORDER] = y[
                        b * ORDER : (b + 1) * ORDER, p * ORDER : (p + 1) * ORDER
                    ]
            build(cos_ref, sin_ref, flip_ref, at + layer + 1, True, wu_ref.at[i])
        for i in range(many):
            at = (first + i) * layers
            y = jnp.dot(wu_ref[i], s_ref[i], preferred_element_type=jnp.float32)
            y = bridge(y).astype(jnp.bfloat16)
            for b in range(blocks):
                for p in range(2):
                    t_refs[i][b * ORDER : (b + 1) * ORDER, p * ORDER : (p + 1) * ORDER] = y[
                        p * ORDER : (p + 1) * ORDER, b * ORDER : (b + 1) * ORDER
                    ]
            build(cos_ref, sin_ref, flip_ref, at + following, False, wl_ref.at[i])
        return carry

    lax.fori_loop(0, layers // 2, two, 0)


def layers_scratch(rows):
    return [
        pltpu.VMEM((GROUP, 2 * ORDER, 2 * ORDER), jnp.bfloat16),
        pltpu.VMEM((GROUP, 2 * ORDER, 2 * ORDER), jnp.bfloat16),
        pltpu.VMEM((GROUP, 2 * ORDER, rows), jnp.bfloat16),
    ]


def layers_kernel(layers, cos_ref, sin_ref, flip_ref, x_ref, t_ref, wl_ref, wu_ref, s_ref):
    first = pl.program_id(0) * GROUP
    run_layers(
        first, layers, cos_ref, sin_ref, flip_ref,
        [x_ref.at[i] for i in range(GROUP)], [t_ref.at[i] for i in range(GROUP)],
        wl_ref, wu_ref, s_ref,
    )


def small_tables(layer_angles, entangler):
    angle = layer_angles.astype(jnp.float32).reshape(-1) * (math.pi / TABLE)
    flip = 1.0 - 2.0 * entangler.astype(jnp.float32).reshape(-1)
    return jnp.cos(angle), jnp.sin(angle), flip


def all_layers(states, layer_angles, entangler):
    circuits, _, local = states.shape
    rows = local // ORDER
    layers = layer_angles.shape[1]
    smem = pl.BlockSpec(memory_space=pltpu.SMEM)
    return pl.pallas_call(
        functools.partial(layers_kernel, layers),
        grid=(circuits // GROUP,),
        out_shape=jax.ShapeDtypeStruct((circuits, rows, 2 * ORDER), jnp.bfloat16),
        in_specs=[smem, smem, smem, pl.BlockSpec((GROUP, 2, rows, ORDER), lambda g: (g, 0, 0, 0))],
        out_specs=pl.BlockSpec((GROUP, rows, 2 * ORDER), lambda g: (g, 0, 0)),
        scratch_shapes=layers_scratch(rows),
        compiler_params=pltpu.CompilerParams(vmem_limit_bytes=32 << 20),
    )(*small_tables(layer_angles, entangler), states.reshape(circuits, 2, rows, ORDER))


MESH_ID = pl.DeviceIdType.MESH


def gate_pair(gate, low, high):
    outs = []
    for r in range(2):
        a_real, a_imag, b_real, b_imag = (gate[4 * r + k : 4 * r + k + 1] for k in range(4))
        real = a_real * low[0] - a_imag * low[1] + (b_real * high[0] - b_imag * high[1])
        imag = a_real * low[1] + a_imag * low[0] + (b_real * high[1] + b_imag * high[0])
        outs.append((real, imag))
    return outs


def fused_kernel(
    layers, ens, amp,
    cos_ref, sin_ref, flip_ref, gate_ref, x_ref, o_ref,
    wl_ref, wu_ref, s_ref, t_ref, r_ref, c_ref, f_ref, h_ref, p_ref, q_ref,
    send_sem, recv_sem, gate_send, gate_recv, sum_send, sum_recv,
):
    circuits, rows, _ = t_ref.shape
    groups = circuits // GROUP
    share = rows // (2 * ens)
    parts = share // 16
    bit = amp.bit_length() - 2
    me = lax.axis_index("ens")
    here = lax.axis_index("amp")
    side = (here // 2**bit) % 2
    rest = here - side * 2**bit

    barrier = pltpu.get_barrier_semaphore()
    everyone = [(k // amp, k % amp) for k in range(1, ens * amp)]
    for e, a in everyone:
        pl.semaphore_signal(
            barrier, inc=1, device_id={"ens": (me + e) % ens, "amp": (here + a) % amp}, device_id_type=MESH_ID
        )
    pl.semaphore_wait(barrier, len(everyone))

    def gate_copy(k, source):
        return pltpu.make_async_remote_copy(
            src_ref=gate_ref,
            dst_ref=c_ref.at[pl.ds(source * circuits, circuits)],
            send_sem=gate_send.at[k - 1],
            recv_sem=gate_recv.at[k - 1],
            device_id={"ens": (me + k) % ens},
            device_id_type=MESH_ID,
        )

    for k in range(1, ens):
        gate_copy(k, me).start()
    c_ref[pl.ds(me * circuits, circuits)] = gate_ref[...]

    peers = [(k // ens, k % ens) for k in range(1, 2 * ens)]

    def piece(k, group, from_side, from_ens):
        across, along = peers[k]
        to_side = side + across - 2 * side * across
        to_ens = (me + along) % ens
        start = pl.multiple_of((to_side * ens + to_ens) * share, share)
        return pltpu.make_async_remote_copy(
            src_ref=t_ref.at[pl.ds(group * GROUP, GROUP), pl.ds(start, share)],
            dst_ref=r_ref.at[from_side, pl.ds(from_ens * circuits + group * GROUP, GROUP)],
            send_sem=send_sem.at[group, k],
            recv_sem=recv_sem.at[group, k],
            device_id={"ens": to_ens, "amp": to_side * 2**bit + rest},
            device_id_type=MESH_ID,
        )

    def compute(group, carry):
        first = group * GROUP
        run_layers(
            first, layers, cos_ref, sin_ref, flip_ref,
            [x_ref.at[first + i] for i in range(GROUP)], [t_ref.at[first + i] for i in range(GROUP)],
            wl_ref, wu_ref, s_ref,
        )
        for k in range(len(peers)):
            piece(k, group, side, me).start()
        own = pl.multiple_of((side * ens + me) * share, share)
        for i in range(GROUP):
            r_ref[side, me * circuits + first + i] = t_ref[first + i, pl.ds(own, share), :]
        return carry

    lax.fori_loop(0, groups, compute, 0)
    for k in range(1, ens):
        gate_copy(k, (me + ens - k) % ens).wait_recv()

    def arrive(group, carry):
        for k, (across, along) in enumerate(peers):
            piece(k, group, side + across - 2 * side * across, (me + ens - along) % ens).wait_recv()

        def one(step, inner):
            which = (step // GROUP) * circuits + group * GROUP + step % GROUP
            gate = c_ref[which]
            low = r_ref[0, which].astype(jnp.float32)
            high = r_ref[1, which].astype(jnp.float32)
            outs = gate_pair(gate, (low[:, :ORDER], low[:, ORDER:]), (high[:, :ORDER], high[:, ORDER:]))
            for x, (real, imag) in enumerate(outs):
                real = real.astype(jnp.bfloat16)
                minus = (-real).astype(jnp.bfloat16)
                imag = imag.astype(jnp.bfloat16)
                for part in range(parts):
                    at = (x * parts + part) * 2 * ORDER
                    take = slice(16 * part, 16 * part + 16)
                    f_ref[which, :, at : at + ORDER] = real[take]
                    f_ref[which, :, at + ORDER : at + 2 * ORDER] = imag[take]
                    h_ref[which, :, at : at + ORDER] = imag[take]
                    h_ref[which, :, at + ORDER : at + 2 * ORDER] = minus[take]
            return inner

        lax.fori_loop(0, ens * GROUP, one, 0)
        return carry

    lax.fori_loop(0, groups, arrive, 0)

    total = ens * circuits
    depth = f_ref.shape[2]
    block = 16
    p_ref[...] = jnp.zeros_like(p_ref)

    def columns(step, carry):
        rhs_at = pl.ds(step * block, block)
        lhs = f_ref[...].reshape(total * 16, depth)
        shape = (1, 16, block * 16)
        same = lax.broadcasted_iota(jnp.int32, shape, 1) == lax.broadcasted_iota(jnp.int32, shape, 2) % 16
        pick_shape = (block * 16, 128)
        pick = lax.broadcasted_iota(jnp.int32, pick_shape, 0) // 16 + step * block
        pick = (pick == lax.broadcasted_iota(jnp.int32, pick_shape, 1)).astype(jnp.float32)
        for which, ref in enumerate((f_ref, h_ref)):
            rhs = ref[rhs_at].reshape(block * 16, depth)
            full = lax.dot_general(lhs, rhs, (((1,), (1,)), ((), ())), preferred_element_type=jnp.float32)
            kept = jnp.where(same, full.reshape(total, 16, block * 16), 0.0).sum(1)
            p_ref[which] += jnp.dot(
                kept, pick, precision=lax.Precision.HIGHEST, preferred_element_type=jnp.float32
            )
        return carry

    lax.fori_loop(0, total // block, columns, 0)

    def slab(k):
        e, a = everyone[k]
        to = (me + e) % ens
        return pltpu.make_async_remote_copy(
            src_ref=p_ref.at[:, pl.ds(pl.multiple_of(to * circuits, circuits), circuits)],
            dst_ref=q_ref.at[k],
            send_sem=sum_send.at[k],
            recv_sem=sum_recv.at[k],
            device_id={"ens": to, "amp": (here + a) % amp},
            device_id_type=MESH_ID,
        )

    for k in range(len(everyone)):
        slab(k).start()
    result = p_ref[:, pl.ds(pl.multiple_of(me * circuits, circuits), circuits), :]
    for k in range(len(everyone)):
        slab(k).wait_recv()
        result = result + q_ref[k]
    o_ref[...] = result
    for k in range(len(everyone)):
        slab(k).wait_send()
    for k in range(1, ens):
        gate_copy(k, me).wait_send()

    def drain(group, carry):
        for k in range(len(peers)):
            piece(k, group, side, me).wait_send()
        return carry

    lax.fori_loop(0, groups, drain, 0)


def fused(states, layer_angles, entangler, global_angles):
    circuits, _, local = states.shape
    rows = local // ORDER
    layers = layer_angles.shape[1]
    ens, amp = lax.axis_size("ens"), lax.axis_size("amp")
    total = ens * circuits
    share = rows // (2 * ens)
    depth = 2 * (share // 16) * 2 * ORDER
    gate = rotation(global_angles[:, 0], global_angles[:, 1])
    coefficients = jnp.stack([part for entry in gate for part in entry], 1)
    coefficients = jnp.broadcast_to(coefficients[:, :, None], (circuits, 8, 128))
    smem = pl.BlockSpec(memory_space=pltpu.SMEM)
    vmem = pl.BlockSpec(memory_space=pltpu.VMEM)
    groups = circuits // GROUP
    return pl.pallas_call(
        functools.partial(fused_kernel, layers, ens, amp),
        out_shape=jax.ShapeDtypeStruct((2, circuits, 128), jnp.float32),
        in_specs=[smem, smem, smem, vmem, vmem],
        out_specs=vmem,
        scratch_shapes=layers_scratch(rows)
        + [
            pltpu.VMEM((circuits, rows, 2 * ORDER), jnp.bfloat16),
            pltpu.VMEM((2, total, share, 2 * ORDER), jnp.bfloat16),
            pltpu.VMEM((total, 8, 128), jnp.float32),
            pltpu.VMEM((total, 16, depth), jnp.bfloat16),
            pltpu.VMEM((total, 16, depth), jnp.bfloat16),
            pltpu.VMEM((2, total, 128), jnp.float32),
            pltpu.VMEM((ens * amp - 1, 2, circuits, 128), jnp.float32),
            pltpu.SemaphoreType.DMA((groups, 2 * ens - 1)),
            pltpu.SemaphoreType.DMA((groups, 2 * ens - 1)),
            pltpu.SemaphoreType.DMA((ens - 1,)),
            pltpu.SemaphoreType.DMA((ens - 1,)),
            pltpu.SemaphoreType.DMA((ens * amp - 1,)),
            pltpu.SemaphoreType.DMA((ens * amp - 1,)),
        ],
        compiler_params=pltpu.CompilerParams(
            vmem_limit_bytes=48 << 20, collective_id=0, has_side_effects=True
        ),
    )(*small_tables(layer_angles, entangler), coefficients, states.reshape(circuits, 2, rows, ORDER))


def finish(summed, states, circuits):
    columns = lax.axis_size("ens") * circuits // lax.axis_size("amp")
    row_index = lax.axis_index("ens") * circuits + jnp.arange(circuits, dtype=jnp.int32)
    column_index = lax.axis_index("amp") * columns + jnp.arange(columns, dtype=jnp.int32)
    off_diagonal = jnp.where(row_index[:, None] == column_index[None, :], 0.0, 1.0).astype(jnp.float32)
    amplitudes = states.shape[2] * lax.axis_size("amp")
    return summed * (off_diagonal / math.sqrt(amplitudes))[None]


def fits(states):
    circuits, _, local = states.shape
    ens = lax.axis_size("ens")
    rows = local // ORDER
    return (
        rows % (2 * ens * 16) == 0 and circuits % 8 == 0 and ens * circuits % 16 == 0
        and ens * circuits <= 128 and lax.axis_size("amp") >= 2 and local <= 1 << 16 and ens > 1
    )


def scaled(coefficient, amplitudes):
    real_c = coefficient[0][:, None]
    imag_c = coefficient[1][:, None]
    return jnp.stack(
        [
            real_c * amplitudes[:, 0] - imag_c * amplitudes[:, 1],
            real_c * amplitudes[:, 1] + imag_c * amplitudes[:, 0],
        ],
        1,
    )


def choose_pair(upper_side, when_lower, when_upper):
    return (
        jnp.where(upper_side == 0, when_lower[0], when_upper[0]),
        jnp.where(upper_side == 0, when_lower[1], when_upper[1]),
    )


def pair_tile(mine, remote):
    products = jnp.einsum("ipa,jqa->pqij", mine, remote, preferred_element_type=jnp.float32)
    return jnp.stack([products[0, 0] + products[1, 1], products[0, 1] - products[1, 0]])


def body(states, layer_angles, entangler, global_angles):
    circuits = states.shape[0]
    if fits(states):
        summed = fused(states, layer_angles, entangler, global_angles)
        columns = lax.axis_size("ens") * circuits // lax.axis_size("amp")
        summed = lax.dynamic_slice_in_dim(summed, lax.axis_index("amp") * columns, columns, 2)
        return finish(summed, states, circuits)
    turned = all_layers(states, layer_angles, entangler).reshape(circuits, -1, 2, ORDER)
    current = jnp.swapaxes(turned, 1, 2).reshape(states.shape)
    swap_bit = lax.axis_size("amp").bit_length() - 2
    upper_side = lax.axis_index("amp") // 2**swap_bit % 2
    gate = rotation(global_angles[:, 0], global_angles[:, 1])
    partner = from_partner(current, "amp", swap_bit)
    coeff_self = choose_pair(upper_side, gate[0], gate[3])
    coeff_other = choose_pair(upper_side, gate[1], gate[2])
    final_states = (
        scaled(coeff_self, current.astype(jnp.float32))
        + scaled(coeff_other, partner.astype(jnp.float32))
    ).astype(jnp.bfloat16)
    partials = pair_tile(final_states, lax.all_gather(final_states, "ens", axis=0, tiled=True))
    summed = lax.psum_scatter(partials, "amp", scatter_dimension=2, tiled=True)
    return finish(summed, states, circuits)


def solution(mesh):
    return jax.shard_map(
        body,
        mesh=mesh,
        in_specs=(
            P(("groups", "ens"), None, "amp"),
            P(("groups", "ens"), None, None, None),
            P(("groups", "ens"), None, None),
            P(("groups", "ens"), None),
        ),
        out_specs=P(None, ("groups", "ens"), "amp"),
        check_vma=False,
    )
```

```python
import functools
import math

import jax
import jax.numpy as jnp
from jax import lax
from jax.experimental import pallas as pl
from jax.experimental.pallas import tpu as pltpu
from jax.sharding import PartitionSpec as P

JOINED = 7
TABLE = 64
ORDER = 2**JOINED
LOW = 3
GROUP = 2


def from_partner(array, axis, bit):
    return lax.ppermute(array, axis, [(i, i ^ 1 << bit) for i in range(lax.axis_size(axis))])


def rotation(polar_index, azimuth_index):
    polar = polar_index.astype(jnp.float32) * (math.pi / TABLE)
    azimuth = azimuth_index.astype(jnp.float32) * (math.pi / TABLE)
    cos_polar = jnp.cos(polar)
    sin_polar = jnp.sin(polar)
    cos_azim = jnp.cos(azimuth)
    sin_azim = jnp.sin(azimuth)
    return (
        (cos_azim * cos_polar, -sin_azim * cos_polar),
        (-cos_azim * sin_polar, sin_azim * sin_polar),
        (cos_azim * sin_polar, sin_azim * sin_polar),
        (cos_azim * cos_polar, sin_azim * cos_polar),
    )


def bit_of(shape, dim, bit, shift=0):
    return (lax.broadcasted_iota(jnp.int32, shape, dim) >> (bit - shift)) & 1


def part_factor(cos_ref, sin_ref, flip_ref, at, upper, high):
    qubits = range(LOW, JOINED) if high else range(LOW)
    shape = (2 ** len(qubits), ORDER)
    shift = LOW if high else 0
    row = {k: bit_of(shape, 0, k, shift) for k in qubits}
    lane = {k: bit_of(shape, 1, k) for k in range(JOINED)}
    out = row if upper else lane
    real = imag = None
    turn = None
    for k in qubits:
        cos_t, sin_t = cos_ref[at * 14 + 2 * k], sin_ref[at * 14 + 2 * k]
        cos_f, sin_f = cos_ref[at * 14 + 2 * k + 1], sin_ref[at * 14 + 2 * k + 1]
        side = (2 * out[k] - 1).astype(jnp.float32)
        factor = jnp.where(row[k] == lane[k], cos_t, side * sin_t)
        turn = factor if turn is None else turn * factor
        step = side * sin_f
        if real is None:
            real, imag = jnp.full(shape, cos_f), step
        else:
            real, imag = real * cos_f - imag * step, real * step + imag * cos_f
    for k in range(JOINED - 1):
        inside = k in qubits and k + 1 in qubits
        if inside or (not upper and not high and k == LOW - 1):
            turn = jnp.where(out[k] * out[k + 1] == 1, flip_ref[at * 6 + k] * turn, turn)
    return real * turn, imag * turn


def build(cos_ref, sin_ref, flip_ref, at, upper, w_ref):
    low_real, low_imag = part_factor(cos_ref, sin_ref, flip_ref, at, upper, False)
    high_real, high_imag = part_factor(cos_ref, sin_ref, flip_ref, at, upper, True)
    lows = [(low_real, low_imag)] * 2
    if upper:
        crossed = bit_of(low_real.shape, 0, LOW - 1) == 1
        flip = flip_ref[at * 6 + LOW - 1]
        lows[1] = tuple(jnp.where(crossed, flip * v, v) for v in lows[0])
    for pair in range(ORDER // 16):
        reals, imags = [], []
        for odd in range(2):
            r = 2 * pair + odd
            a_real = jnp.broadcast_to(high_real[r : r + 1], (8, ORDER))
            a_imag = jnp.broadcast_to(high_imag[r : r + 1], (8, ORDER))
            b_real, b_imag = lows[odd]
            reals.append(a_real * b_real - a_imag * b_imag)
            imags.append(a_real * b_imag + a_imag * b_real)
        real = jnp.concatenate(reals, 0)
        imag = jnp.concatenate(imags, 0)
        plus, minus = imag.astype(jnp.bfloat16), (-imag).astype(jnp.bfloat16)
        real = real.astype(jnp.bfloat16)
        top, bottom = (minus, plus) if upper else (plus, minus)
        rows = pl.ds(16 * pair, 16)
        rows_below = pl.ds(ORDER + 16 * pair, 16)
        w_ref[rows, :ORDER] = real
        w_ref[rows, ORDER:] = top
        w_ref[rows_below, :ORDER] = bottom
        w_ref[rows_below, ORDER:] = real


def bridge(values):
    rows, columns = values.shape
    shape = (1, 8, columns)
    odd = bit_of(shape, 1, 0) * bit_of(shape, 2, JOINED - 1)
    sign = (1 - 2 * odd).astype(jnp.float32)
    return (values.reshape(rows // 8, 8, columns) * sign).reshape(rows, columns)


def run_layers(first, layers, cos_ref, sin_ref, flip_ref, x_refs, t_refs, wl_ref, wu_ref, s_ref):
    rows = t_refs[0].shape[0]
    blocks = rows // ORDER
    many = len(t_refs)
    for i in range(many):
        t_refs[i][:, :ORDER] = x_refs[i][0]
        t_refs[i][:, ORDER:] = x_refs[i][1]
        build(cos_ref, sin_ref, flip_ref, (first + i) * layers, False, wl_ref.at[i])

    def two(pair, carry):
        layer = 2 * pair
        following = jnp.minimum(layer + 2, layers - 2)
        for i in range(many):
            at = (first + i) * layers
            y = jnp.dot(t_refs[i][...], wl_ref[i], preferred_element_type=jnp.float32)
            y = bridge(y).astype(jnp.bfloat16)
            for b in range(blocks):
                for p in range(2):
                    s_ref[i, p * ORDER : (p + 1) * ORDER, b * ORDER : (b + 1) * ORDER] = y[
                        b * ORDER : (b + 1) * ORDER, p * ORDER : (p + 1) * ORDER
                    ]
            build(cos_ref, sin_ref, flip_ref, at + layer + 1, True, wu_ref.at[i])
        for i in range(many):
            at = (first + i) * layers
            y = jnp.dot(wu_ref[i], s_ref[i], preferred_element_type=jnp.float32)
            y = bridge(y).astype(jnp.bfloat16)
            for b in range(blocks):
                for p in range(2):
                    t_refs[i][b * ORDER : (b + 1) * ORDER, p * ORDER : (p + 1) * ORDER] = y[
                        p * ORDER : (p + 1) * ORDER, b * ORDER : (b + 1) * ORDER
                    ]
            build(cos_ref, sin_ref, flip_ref, at + following, False, wl_ref.at[i])
        return carry

    lax.fori_loop(0, layers // 2, two, 0)


def layers_scratch(rows):
    return [
        pltpu.VMEM((GROUP, 2 * ORDER, 2 * ORDER), jnp.bfloat16),
        pltpu.VMEM((GROUP, 2 * ORDER, 2 * ORDER), jnp.bfloat16),
        pltpu.VMEM((GROUP, 2 * ORDER, rows), jnp.bfloat16),
    ]


def layers_kernel(layers, cos_ref, sin_ref, flip_ref, x_ref, t_ref, wl_ref, wu_ref, s_ref):
    first = pl.program_id(0) * GROUP
    run_layers(
        first, layers, cos_ref, sin_ref, flip_ref,
        [x_ref.at[i] for i in range(GROUP)], [t_ref.at[i] for i in range(GROUP)],
        wl_ref, wu_ref, s_ref,
    )


def small_tables(layer_angles, entangler):
    angle = layer_angles.astype(jnp.float32).reshape(-1) * (math.pi / TABLE)
    flip = 1.0 - 2.0 * entangler.astype(jnp.float32).reshape(-1)
    return jnp.cos(angle), jnp.sin(angle), flip


def all_layers(states, layer_angles, entangler):
    circuits, _, local = states.shape
    rows = local // ORDER
    layers = layer_angles.shape[1]
    smem = pl.BlockSpec(memory_space=pltpu.SMEM)
    return pl.pallas_call(
        functools.partial(layers_kernel, layers),
        grid=(circuits // GROUP,),
        out_shape=jax.ShapeDtypeStruct((circuits, rows, 2 * ORDER), jnp.bfloat16),
        in_specs=[smem, smem, smem, pl.BlockSpec((GROUP, 2, rows, ORDER), lambda g: (g, 0, 0, 0))],
        out_specs=pl.BlockSpec((GROUP, rows, 2 * ORDER), lambda g: (g, 0, 0)),
        scratch_shapes=layers_scratch(rows),
        compiler_params=pltpu.CompilerParams(vmem_limit_bytes=32 << 20),
    )(*small_tables(layer_angles, entangler), states.reshape(circuits, 2, rows, ORDER))


MESH_ID = pl.DeviceIdType.MESH


def gate_pair(gate, low, high):
    outs = []
    for r in range(2):
        a_real, a_imag, b_real, b_imag = (gate[4 * r + k : 4 * r + k + 1] for k in range(4))
        real = a_real * low[0] - a_imag * low[1] + (b_real * high[0] - b_imag * high[1])
        imag = a_real * low[1] + a_imag * low[0] + (b_real * high[1] + b_imag * high[0])
        outs.append((real, imag))
    return outs


def fused_kernel(
    layers, ens, amp,
    cos_ref, sin_ref, flip_ref, gate_ref, x_ref, o_ref,
    wl_ref, wu_ref, s_ref, t_ref, r_ref, c_ref, f_ref, h_ref, l_ref, p_ref, q_ref,
    send_sem, recv_sem, gate_send, gate_recv, sum_send, sum_recv,
):
    circuits, rows, _ = t_ref.shape
    groups = circuits // GROUP
    share = rows // (2 * ens)
    parts = share // 16
    bit = amp.bit_length() - 2
    me = lax.axis_index("ens")
    here = lax.axis_index("amp")
    side = (here // 2**bit) % 2
    rest = here - side * 2**bit

    barrier = pltpu.get_barrier_semaphore()
    everyone = [(k // amp, k % amp) for k in range(1, ens * amp)]
    for e, a in everyone:
        pl.semaphore_signal(
            barrier, inc=1, device_id={"ens": (me + e) % ens, "amp": (here + a) % amp}, device_id_type=MESH_ID
        )
    pl.semaphore_wait(barrier, len(everyone))

    def gate_copy(k, source):
        return pltpu.make_async_remote_copy(
            src_ref=gate_ref,
            dst_ref=c_ref.at[pl.ds(source * circuits, circuits)],
            send_sem=gate_send.at[k - 1],
            recv_sem=gate_recv.at[k - 1],
            device_id={"ens": (me + k) % ens},
            device_id_type=MESH_ID,
        )

    for k in range(1, ens):
        gate_copy(k, me).start()
    c_ref[pl.ds(me * circuits, circuits)] = gate_ref[...]

    peers = [(k // ens, k % ens) for k in range(1, 2 * ens)]

    def piece(k, group, from_side, from_ens):
        across, along = peers[k]
        to_side = side + across - 2 * side * across
        to_ens = (me + along) % ens
        start = pl.multiple_of((to_side * ens + to_ens) * share, share)
        return pltpu.make_async_remote_copy(
            src_ref=t_ref.at[pl.ds(group * GROUP, GROUP), pl.ds(start, share)],
            dst_ref=r_ref.at[from_side, pl.ds(from_ens * circuits + group * GROUP, GROUP)],
            send_sem=send_sem.at[group, k],
            recv_sem=recv_sem.at[group, k],
            device_id={"ens": to_ens, "amp": to_side * 2**bit + rest},
            device_id_type=MESH_ID,
        )

    def compute(group, carry):
        first = group * GROUP
        run_layers(
            first, layers, cos_ref, sin_ref, flip_ref,
            [x_ref.at[first + i] for i in range(GROUP)], [t_ref.at[first + i] for i in range(GROUP)],
            wl_ref, wu_ref, s_ref,
        )
        for k in range(len(peers)):
            piece(k, group, side, me).start()
        own = pl.multiple_of((side * ens + me) * share, share)
        for i in range(GROUP):
            r_ref[side, me * circuits + first + i] = t_ref[first + i, pl.ds(own, share), :]
        return carry

    lax.fori_loop(0, groups, compute, 0)
    for k in range(1, ens):
        gate_copy(k, (me + ens - k) % ens).wait_recv()

    total = ens * circuits
    fresh = ens * GROUP
    depth = f_ref.shape[2]
    l_ref[...] = jnp.zeros_like(l_ref)

    for group in range(groups):
        for k, (across, along) in enumerate(peers):
            piece(k, group, side + across - 2 * side * across, (me + ens - along) % ens).wait_recv()

        def one(step, inner, group=group):
            which = (step // GROUP) * circuits + group * GROUP + step % GROUP
            gate = c_ref[which]
            low = r_ref[0, which].astype(jnp.float32)
            high = r_ref[1, which].astype(jnp.float32)
            outs = gate_pair(gate, (low[:, :ORDER], low[:, ORDER:]), (high[:, :ORDER], high[:, ORDER:]))
            for x, (real, imag) in enumerate(outs):
                real = real.astype(jnp.bfloat16)
                minus = (-real).astype(jnp.bfloat16)
                imag = imag.astype(jnp.bfloat16)
                for part in range(parts):
                    at = (x * parts + part) * 2 * ORDER
                    take = slice(16 * part, 16 * part + 16)
                    for ref, row in ((f_ref, group * fresh + step), (h_ref, step)):
                        ref[row, :, at : at + ORDER] = real[take]
                        ref[row, :, at + ORDER : at + 2 * ORDER] = imag[take]
                    h_ref[fresh + step, :, at : at + ORDER] = imag[take]
                    h_ref[fresh + step, :, at + ORDER : at + 2 * ORDER] = minus[take]
            return inner

        lax.fori_loop(0, fresh, one, 0)
        known = (group + 1) * fresh
        lhs = f_ref[:known].reshape(known * 16, depth)
        rhs = h_ref[...].reshape(2 * fresh * 16, depth)
        full = lax.dot_general(lhs, rhs, (((1,), (1,)), ((), ())), preferred_element_type=jnp.float32)
        shape = (1, 16, 2 * fresh * 16)
        same = lax.broadcasted_iota(jnp.int32, shape, 1) == lax.broadcasted_iota(jnp.int32, shape, 2) % 16
        kept = jnp.where(same, full.reshape(known, 16, 2 * fresh * 16), 0.0).sum(1)
        pick_shape = (fresh * 16, 128)
        pick = lax.broadcasted_iota(jnp.int32, pick_shape, 0) // 16 + group * fresh
        pick = (pick == lax.broadcasted_iota(jnp.int32, pick_shape, 1)).astype(jnp.float32)
        for which in range(2):
            l_ref[which, :known] += jnp.dot(
                kept[:, which * fresh * 16 : (which + 1) * fresh * 16], pick,
                precision=lax.Precision.HIGHEST, preferred_element_type=jnp.float32,
            )

    square = (128, 128)
    row = lax.broadcasted_iota(jnp.int32, square, 0)
    column = lax.broadcasted_iota(jnp.int32, square, 1)
    place = (row % circuits // GROUP) * fresh + row // circuits * GROUP + row % GROUP
    order = jnp.where((place == column) & (row < total), 1.0, 0.0)
    for which in range(2):
        half = l_ref[which]
        above = jnp.where(row // fresh < column // fresh, half, 0.0)
        mirrored = jnp.transpose(above)
        whole = half + mirrored if which == 0 else half - mirrored
        moved = jnp.dot(order, whole, precision=lax.Precision.HIGHEST, preferred_element_type=jnp.float32)
        p_ref[which] = lax.dot_general(
            moved, order, (((1,), (1,)), ((), ())),
            precision=lax.Precision.HIGHEST, preferred_element_type=jnp.float32,
        )[:total]

    def slab(k):
        e, a = everyone[k]
        to = (me + e) % ens
        return pltpu.make_async_remote_copy(
            src_ref=p_ref.at[:, pl.ds(pl.multiple_of(to * circuits, circuits), circuits)],
            dst_ref=q_ref.at[k],
            send_sem=sum_send.at[k],
            recv_sem=sum_recv.at[k],
            device_id={"ens": to, "amp": (here + a) % amp},
            device_id_type=MESH_ID,
        )

    for k in range(len(everyone)):
        slab(k).start()
    result = p_ref[:, pl.ds(pl.multiple_of(me * circuits, circuits), circuits), :]
    for k in range(len(everyone)):
        slab(k).wait_recv()
        result = result + q_ref[k]
    o_ref[...] = result
    for k in range(len(everyone)):
        slab(k).wait_send()
    for k in range(1, ens):
        gate_copy(k, me).wait_send()

    def drain(group, carry):
        for k in range(len(peers)):
            piece(k, group, side, me).wait_send()
        return carry

    lax.fori_loop(0, groups, drain, 0)


def fused(states, layer_angles, entangler, global_angles):
    circuits, _, local = states.shape
    rows = local // ORDER
    layers = layer_angles.shape[1]
    ens, amp = lax.axis_size("ens"), lax.axis_size("amp")
    total = ens * circuits
    share = rows // (2 * ens)
    depth = 2 * (share // 16) * 2 * ORDER
    gate = rotation(global_angles[:, 0], global_angles[:, 1])
    coefficients = jnp.stack([part for entry in gate for part in entry], 1)
    coefficients = jnp.broadcast_to(coefficients[:, :, None], (circuits, 8, 128))
    smem = pl.BlockSpec(memory_space=pltpu.SMEM)
    vmem = pl.BlockSpec(memory_space=pltpu.VMEM)
    groups = circuits // GROUP
    return pl.pallas_call(
        functools.partial(fused_kernel, layers, ens, amp),
        out_shape=jax.ShapeDtypeStruct((2, circuits, 128), jnp.float32),
        in_specs=[smem, smem, smem, vmem, vmem],
        out_specs=vmem,
        scratch_shapes=layers_scratch(rows)
        + [
            pltpu.VMEM((circuits, rows, 2 * ORDER), jnp.bfloat16),
            pltpu.VMEM((2, total, share, 2 * ORDER), jnp.bfloat16),
            pltpu.VMEM((total, 8, 128), jnp.float32),
            pltpu.VMEM((total, 16, depth), jnp.bfloat16),
            pltpu.VMEM((2 * ens * GROUP, 16, depth), jnp.bfloat16),
            pltpu.VMEM((2, 128, 128), jnp.float32),
            pltpu.VMEM((2, total, 128), jnp.float32),
            pltpu.VMEM((ens * amp - 1, 2, circuits, 128), jnp.float32),
            pltpu.SemaphoreType.DMA((groups, 2 * ens - 1)),
            pltpu.SemaphoreType.DMA((groups, 2 * ens - 1)),
            pltpu.SemaphoreType.DMA((ens - 1,)),
            pltpu.SemaphoreType.DMA((ens - 1,)),
            pltpu.SemaphoreType.DMA((ens * amp - 1,)),
            pltpu.SemaphoreType.DMA((ens * amp - 1,)),
        ],
        compiler_params=pltpu.CompilerParams(
            vmem_limit_bytes=48 << 20, collective_id=0, has_side_effects=True
        ),
    )(*small_tables(layer_angles, entangler), coefficients, states.reshape(circuits, 2, rows, ORDER))


def finish(summed, states, circuits):
    columns = lax.axis_size("ens") * circuits // lax.axis_size("amp")
    row_index = lax.axis_index("ens") * circuits + jnp.arange(circuits, dtype=jnp.int32)
    column_index = lax.axis_index("amp") * columns + jnp.arange(columns, dtype=jnp.int32)
    off_diagonal = jnp.where(row_index[:, None] == column_index[None, :], 0.0, 1.0).astype(jnp.float32)
    amplitudes = states.shape[2] * lax.axis_size("amp")
    return summed * (off_diagonal / math.sqrt(amplitudes))[None]


def fits(states):
    circuits, _, local = states.shape
    ens = lax.axis_size("ens")
    rows = local // ORDER
    return (
        rows % (2 * ens * 16) == 0 and circuits % 8 == 0 and ens * circuits % 16 == 0
        and ens * circuits <= 128 and lax.axis_size("amp") >= 2 and local <= 1 << 16 and ens > 1
    )


def scaled(coefficient, amplitudes):
    real_c = coefficient[0][:, None]
    imag_c = coefficient[1][:, None]
    return jnp.stack(
        [
            real_c * amplitudes[:, 0] - imag_c * amplitudes[:, 1],
            real_c * amplitudes[:, 1] + imag_c * amplitudes[:, 0],
        ],
        1,
    )


def choose_pair(upper_side, when_lower, when_upper):
    return (
        jnp.where(upper_side == 0, when_lower[0], when_upper[0]),
        jnp.where(upper_side == 0, when_lower[1], when_upper[1]),
    )


def pair_tile(mine, remote):
    products = jnp.einsum("ipa,jqa->pqij", mine, remote, preferred_element_type=jnp.float32)
    return jnp.stack([products[0, 0] + products[1, 1], products[0, 1] - products[1, 0]])


def body(states, layer_angles, entangler, global_angles):
    circuits = states.shape[0]
    if fits(states):
        summed = fused(states, layer_angles, entangler, global_angles)
        columns = lax.axis_size("ens") * circuits // lax.axis_size("amp")
        summed = lax.dynamic_slice_in_dim(summed, lax.axis_index("amp") * columns, columns, 2)
        return finish(summed, states, circuits)
    turned = all_layers(states, layer_angles, entangler).reshape(circuits, -1, 2, ORDER)
    current = jnp.swapaxes(turned, 1, 2).reshape(states.shape)
    swap_bit = lax.axis_size("amp").bit_length() - 2
    upper_side = lax.axis_index("amp") // 2**swap_bit % 2
    gate = rotation(global_angles[:, 0], global_angles[:, 1])
    partner = from_partner(current, "amp", swap_bit)
    coeff_self = choose_pair(upper_side, gate[0], gate[3])
    coeff_other = choose_pair(upper_side, gate[1], gate[2])
    final_states = (
        scaled(coeff_self, current.astype(jnp.float32))
        + scaled(coeff_other, partner.astype(jnp.float32))
    ).astype(jnp.bfloat16)
    partials = pair_tile(final_states, lax.all_gather(final_states, "ens", axis=0, tiled=True))
    summed = lax.psum_scatter(partials, "amp", scatter_dimension=2, tiled=True)
    return finish(summed, states, circuits)


def solution(mesh):
    return jax.shard_map(
        body,
        mesh=mesh,
        in_specs=(
            P(("groups", "ens"), None, "amp"),
            P(("groups", "ens"), None, None, None),
            P(("groups", "ens"), None, None),
            P(("groups", "ens"), None),
        ),
        out_specs=P(None, ("groups", "ens"), "amp"),
        check_vma=False,
    )
```

```python
import functools
import math

import jax
import jax.numpy as jnp
from jax import lax
from jax.experimental import pallas as pl
from jax.experimental.pallas import tpu as pltpu
from jax.sharding import PartitionSpec as P

JOINED = 7
TABLE = 64
ORDER = 2**JOINED
LOW = 3
GROUP = 1


def from_partner(array, axis, bit):
    return lax.ppermute(array, axis, [(i, i ^ 1 << bit) for i in range(lax.axis_size(axis))])


def rotation(polar_index, azimuth_index):
    polar = polar_index.astype(jnp.float32) * (math.pi / TABLE)
    azimuth = azimuth_index.astype(jnp.float32) * (math.pi / TABLE)
    cos_polar = jnp.cos(polar)
    sin_polar = jnp.sin(polar)
    cos_azim = jnp.cos(azimuth)
    sin_azim = jnp.sin(azimuth)
    return (
        (cos_azim * cos_polar, -sin_azim * cos_polar),
        (-cos_azim * sin_polar, sin_azim * sin_polar),
        (cos_azim * sin_polar, sin_azim * sin_polar),
        (cos_azim * cos_polar, sin_azim * cos_polar),
    )


def bit_of(shape, dim, bit, shift=0):
    return (lax.broadcasted_iota(jnp.int32, shape, dim) >> (bit - shift)) & 1


def part_factor(cos_ref, sin_ref, flip_ref, at, upper, high):
    qubits = range(LOW, JOINED) if high else range(LOW)
    shape = (2 ** len(qubits), ORDER)
    shift = LOW if high else 0
    row = {k: bit_of(shape, 0, k, shift) for k in qubits}
    lane = {k: bit_of(shape, 1, k) for k in range(JOINED)}
    out = row if upper else lane
    real = imag = None
    turn = None
    for k in qubits:
        cos_t, sin_t = cos_ref[at * 14 + 2 * k], sin_ref[at * 14 + 2 * k]
        cos_f, sin_f = cos_ref[at * 14 + 2 * k + 1], sin_ref[at * 14 + 2 * k + 1]
        side = (2 * out[k] - 1).astype(jnp.float32)
        factor = jnp.where(row[k] == lane[k], cos_t, side * sin_t)
        turn = factor if turn is None else turn * factor
        step = side * sin_f
        if real is None:
            real, imag = jnp.full(shape, cos_f), step
        else:
            real, imag = real * cos_f - imag * step, real * step + imag * cos_f
    for k in range(JOINED - 1):
        inside = k in qubits and k + 1 in qubits
        if inside or (not upper and not high and k == LOW - 1):
            turn = jnp.where(out[k] * out[k + 1] == 1, flip_ref[at * 6 + k] * turn, turn)
    return real * turn, imag * turn


def build(cos_ref, sin_ref, flip_ref, at, upper, w_ref):
    low_real, low_imag = part_factor(cos_ref, sin_ref, flip_ref, at, upper, False)
    high_real, high_imag = part_factor(cos_ref, sin_ref, flip_ref, at, upper, True)
    lows = [(low_real, low_imag)] * 2
    if upper:
        crossed = bit_of(low_real.shape, 0, LOW - 1) == 1
        flip = flip_ref[at * 6 + LOW - 1]
        lows[1] = tuple(jnp.where(crossed, flip * v, v) for v in lows[0])
    for pair in range(ORDER // 16):
        reals, imags = [], []
        for odd in range(2):
            r = 2 * pair + odd
            a_real = jnp.broadcast_to(high_real[r : r + 1], (8, ORDER))
            a_imag = jnp.broadcast_to(high_imag[r : r + 1], (8, ORDER))
            b_real, b_imag = lows[odd]
            reals.append(a_real * b_real - a_imag * b_imag)
            imags.append(a_real * b_imag + a_imag * b_real)
        real = jnp.concatenate(reals, 0)
        imag = jnp.concatenate(imags, 0)
        plus, minus = imag.astype(jnp.bfloat16), (-imag).astype(jnp.bfloat16)
        real = real.astype(jnp.bfloat16)
        top, bottom = (minus, plus) if upper else (plus, minus)
        rows = pl.ds(16 * pair, 16)
        rows_below = pl.ds(ORDER + 16 * pair, 16)
        w_ref[rows, :ORDER] = real
        w_ref[rows, ORDER:] = top
        w_ref[rows_below, :ORDER] = bottom
        w_ref[rows_below, ORDER:] = real


def bridge(values):
    rows, columns = values.shape
    shape = (1, 8, columns)
    odd = bit_of(shape, 1, 0) * bit_of(shape, 2, JOINED - 1)
    sign = (1 - 2 * odd).astype(jnp.float32)
    return (values.reshape(rows // 8, 8, columns) * sign).reshape(rows, columns)


def run_layers(first, layers, cos_ref, sin_ref, flip_ref, x_refs, t_refs, wl_ref, wu_ref, s_ref):
    rows = t_refs[0].shape[0]
    blocks = rows // ORDER
    many = len(t_refs)
    for i in range(many):

        def spread(step, carry, i=i):
            flat = x_refs[i][:, pl.ds(pl.multiple_of(step * 16 * ORDER, 16 * ORDER), 16 * ORDER)]
            tiles = flat.astype(jnp.float32).reshape(2, 16, ORDER).astype(jnp.bfloat16)
            rows_at = pl.ds(pl.multiple_of(step * 16, 16), 16)
            t_refs[i][rows_at, :ORDER] = tiles[0]
            t_refs[i][rows_at, ORDER:] = tiles[1]
            return carry

        lax.fori_loop(0, rows // 16, spread, 0, unroll=4)
        build(cos_ref, sin_ref, flip_ref, (first + i) * layers, False, wl_ref.at[i])

    def two(pair, carry):
        layer = 2 * pair
        following = jnp.minimum(layer + 2, layers - 2)
        for i in range(many):
            at = (first + i) * layers
            y = jnp.dot(t_refs[i][...], wl_ref[i], preferred_element_type=jnp.float32)
            y = bridge(y).astype(jnp.bfloat16)
            for b in range(blocks):
                for p in range(2):
                    s_ref[i, p * ORDER : (p + 1) * ORDER, b * ORDER : (b + 1) * ORDER] = y[
                        b * ORDER : (b + 1) * ORDER, p * ORDER : (p + 1) * ORDER
                    ]
            build(cos_ref, sin_ref, flip_ref, at + layer + 1, True, wu_ref.at[i])
        for i in range(many):
            at = (first + i) * layers
            y = jnp.dot(wu_ref[i], s_ref[i], preferred_element_type=jnp.float32)
            y = bridge(y).astype(jnp.bfloat16)
            for b in range(blocks):
                for p in range(2):
                    t_refs[i][b * ORDER : (b + 1) * ORDER, p * ORDER : (p + 1) * ORDER] = y[
                        p * ORDER : (p + 1) * ORDER, b * ORDER : (b + 1) * ORDER
                    ]
            build(cos_ref, sin_ref, flip_ref, at + following, False, wl_ref.at[i])
        return carry

    lax.fori_loop(0, layers // 2, two, 0)


def layers_scratch(rows):
    return [
        pltpu.VMEM((GROUP, 2 * ORDER, 2 * ORDER), jnp.bfloat16),
        pltpu.VMEM((GROUP, 2 * ORDER, 2 * ORDER), jnp.bfloat16),
        pltpu.VMEM((GROUP, 2 * ORDER, rows), jnp.bfloat16),
    ]


def layers_kernel(layers, cos_ref, sin_ref, flip_ref, x_ref, t_ref, wl_ref, wu_ref, s_ref):
    first = pl.program_id(0) * GROUP
    run_layers(
        first, layers, cos_ref, sin_ref, flip_ref,
        [x_ref.at[i] for i in range(GROUP)], [t_ref.at[i] for i in range(GROUP)],
        wl_ref, wu_ref, s_ref,
    )


def small_tables(layer_angles, entangler):
    angle = layer_angles.astype(jnp.float32).reshape(-1) * (math.pi / TABLE)
    flip = 1.0 - 2.0 * entangler.astype(jnp.float32).reshape(-1)
    return jnp.cos(angle), jnp.sin(angle), flip


def all_layers(states, layer_angles, entangler):
    circuits, _, local = states.shape
    rows = local // ORDER
    layers = layer_angles.shape[1]
    smem = pl.BlockSpec(memory_space=pltpu.SMEM)
    return pl.pallas_call(
        functools.partial(layers_kernel, layers),
        grid=(circuits // GROUP,),
        out_shape=jax.ShapeDtypeStruct((circuits, rows, 2 * ORDER), jnp.bfloat16),
        in_specs=[smem, smem, smem, pl.BlockSpec((GROUP, 2, local), lambda g: (g, 0, 0))],
        out_specs=pl.BlockSpec((GROUP, rows, 2 * ORDER), lambda g: (g, 0, 0)),
        scratch_shapes=layers_scratch(rows),
        compiler_params=pltpu.CompilerParams(vmem_limit_bytes=32 << 20),
    )(*small_tables(layer_angles, entangler), states)


MESH_ID = pl.DeviceIdType.MESH


def gate_pair(gate, low, high):
    outs = []
    for r in range(2):
        a_real, a_imag, b_real, b_imag = (gate[4 * r + k : 4 * r + k + 1] for k in range(4))
        real = a_real * low[0] - a_imag * low[1] + (b_real * high[0] - b_imag * high[1])
        imag = a_real * low[1] + a_imag * low[0] + (b_real * high[1] + b_imag * high[0])
        outs.append((real, imag))
    return outs


def fused_kernel(
    layers, ens, amp,
    cos_ref, sin_ref, flip_ref, gate_ref, x_ref, o_ref,
    wl_ref, wu_ref, s_ref, t_ref, r_ref, c_ref, f_ref, h_ref, l_ref, p_ref, q_ref,
    send_sem, recv_sem, gate_send, gate_recv, sum_send, sum_recv,
):
    circuits, rows, _ = t_ref.shape
    groups = circuits // GROUP
    share = rows // (2 * ens)
    parts = share // 16
    bit = amp.bit_length() - 2
    me = lax.axis_index("ens")
    here = lax.axis_index("amp")
    side = (here // 2**bit) % 2
    rest = here - side * 2**bit

    barrier = pltpu.get_barrier_semaphore()
    everyone = [(k // amp, k % amp) for k in range(1, ens * amp)]
    for e, a in everyone:
        pl.semaphore_signal(
            barrier, inc=1, device_id={"ens": (me + e) % ens, "amp": (here + a) % amp}, device_id_type=MESH_ID
        )
    pl.semaphore_wait(barrier, len(everyone))

    def gate_copy(k, source):
        return pltpu.make_async_remote_copy(
            src_ref=gate_ref,
            dst_ref=c_ref.at[pl.ds(source * circuits, circuits)],
            send_sem=gate_send.at[k - 1],
            recv_sem=gate_recv.at[k - 1],
            device_id={"ens": (me + k) % ens},
            device_id_type=MESH_ID,
        )

    for k in range(1, ens):
        gate_copy(k, me).start()
    c_ref[pl.ds(me * circuits, circuits)] = gate_ref[...]

    peers = [(k // ens, k % ens) for k in range(1, 2 * ens)]

    def piece(k, group, from_side, from_ens):
        across, along = peers[k]
        to_side = side + across - 2 * side * across
        to_ens = (me + along) % ens
        start = pl.multiple_of((to_side * ens + to_ens) * share, share)
        return pltpu.make_async_remote_copy(
            src_ref=t_ref.at[pl.ds(group * GROUP, GROUP), pl.ds(start, share)],
            dst_ref=r_ref.at[from_side, pl.ds(from_ens * circuits + group * GROUP, GROUP)],
            send_sem=send_sem.at[group, k],
            recv_sem=recv_sem.at[group, k],
            device_id={"ens": to_ens, "amp": to_side * 2**bit + rest},
            device_id_type=MESH_ID,
        )

    def compute(group, carry):
        first = group * GROUP
        run_layers(
            first, layers, cos_ref, sin_ref, flip_ref,
            [x_ref.at[first + i] for i in range(GROUP)], [t_ref.at[first + i] for i in range(GROUP)],
            wl_ref, wu_ref, s_ref,
        )
        for k in range(len(peers)):
            piece(k, group, side, me).start()
        own = pl.multiple_of((side * ens + me) * share, share)
        for i in range(GROUP):
            r_ref[side, me * circuits + first + i] = t_ref[first + i, pl.ds(own, share), :]
        return carry

    lax.fori_loop(0, groups, compute, 0)
    for k in range(1, ens):
        gate_copy(k, (me + ens - k) % ens).wait_recv()

    total = ens * circuits
    fresh = ens * GROUP
    depth = f_ref.shape[2]
    l_ref[...] = jnp.zeros_like(l_ref)

    for group in range(groups):
        for k, (across, along) in enumerate(peers):
            piece(k, group, side + across - 2 * side * across, (me + ens - along) % ens).wait_recv()

        def one(step, inner, group=group):
            which = (step // GROUP) * circuits + group * GROUP + step % GROUP
            gate = c_ref[which]
            low = r_ref[0, which].astype(jnp.float32)
            high = r_ref[1, which].astype(jnp.float32)
            outs = gate_pair(gate, (low[:, :ORDER], low[:, ORDER:]), (high[:, :ORDER], high[:, ORDER:]))
            for x, (real, imag) in enumerate(outs):
                real = real.astype(jnp.bfloat16)
                minus = (-real).astype(jnp.bfloat16)
                imag = imag.astype(jnp.bfloat16)
                for part in range(parts):
                    at = (x * parts + part) * 2 * ORDER
                    take = slice(16 * part, 16 * part + 16)
                    for ref, row in ((f_ref, group * fresh + step), (h_ref, step)):
                        ref[row, :, at : at + ORDER] = real[take]
                        ref[row, :, at + ORDER : at + 2 * ORDER] = imag[take]
                    h_ref[fresh + step, :, at : at + ORDER] = imag[take]
                    h_ref[fresh + step, :, at + ORDER : at + 2 * ORDER] = minus[take]
            return inner

        lax.fori_loop(0, fresh, one, 0)
        known = (group + 1) * fresh
        lhs = f_ref[:known].reshape(known * 16, depth)
        rhs = h_ref[...].reshape(2 * fresh * 16, depth)
        full = lax.dot_general(lhs, rhs, (((1,), (1,)), ((), ())), preferred_element_type=jnp.float32)
        shape = (1, 16, 2 * fresh * 16)
        same = lax.broadcasted_iota(jnp.int32, shape, 1) == lax.broadcasted_iota(jnp.int32, shape, 2) % 16
        kept = jnp.where(same, full.reshape(known, 16, 2 * fresh * 16), 0.0).sum(1)
        pick_shape = (fresh * 16, 128)
        pick = lax.broadcasted_iota(jnp.int32, pick_shape, 0) // 16 + group * fresh
        pick = (pick == lax.broadcasted_iota(jnp.int32, pick_shape, 1)).astype(jnp.float32)
        for which in range(2):
            l_ref[which, :known] += jnp.dot(
                kept[:, which * fresh * 16 : (which + 1) * fresh * 16], pick,
                precision=lax.Precision.HIGHEST, preferred_element_type=jnp.float32,
            )

    square = (128, 128)
    row = lax.broadcasted_iota(jnp.int32, square, 0)
    column = lax.broadcasted_iota(jnp.int32, square, 1)
    place = (row % circuits // GROUP) * fresh + row // circuits * GROUP + row % GROUP
    order = jnp.where((place == column) & (row < total), 1.0, 0.0)
    for which in range(2):
        half = l_ref[which]
        above = jnp.where(row // fresh < column // fresh, half, 0.0)
        mirrored = jnp.transpose(above)
        whole = half + mirrored if which == 0 else half - mirrored
        moved = jnp.dot(order, whole, precision=lax.Precision.HIGHEST, preferred_element_type=jnp.float32)
        p_ref[which] = lax.dot_general(
            moved, order, (((1,), (1,)), ((), ())),
            precision=lax.Precision.HIGHEST, preferred_element_type=jnp.float32,
        )[:total]

    def slab(k):
        e, a = everyone[k]
        to = (me + e) % ens
        return pltpu.make_async_remote_copy(
            src_ref=p_ref.at[:, pl.ds(pl.multiple_of(to * circuits, circuits), circuits)],
            dst_ref=q_ref.at[k],
            send_sem=sum_send.at[k],
            recv_sem=sum_recv.at[k],
            device_id={"ens": to, "amp": (here + a) % amp},
            device_id_type=MESH_ID,
        )

    for k in range(len(everyone)):
        slab(k).start()
    result = p_ref[:, pl.ds(pl.multiple_of(me * circuits, circuits), circuits), :]
    for k in range(len(everyone)):
        slab(k).wait_recv()
        result = result + q_ref[k]
    o_ref[...] = result
    for k in range(len(everyone)):
        slab(k).wait_send()
    for k in range(1, ens):
        gate_copy(k, me).wait_send()

    def drain(group, carry):
        for k in range(len(peers)):
            piece(k, group, side, me).wait_send()
        return carry

    lax.fori_loop(0, groups, drain, 0)


def fused(states, layer_angles, entangler, global_angles):
    circuits, _, local = states.shape
    rows = local // ORDER
    layers = layer_angles.shape[1]
    ens, amp = lax.axis_size("ens"), lax.axis_size("amp")
    total = ens * circuits
    share = rows // (2 * ens)
    depth = 2 * (share // 16) * 2 * ORDER
    gate = rotation(global_angles[:, 0], global_angles[:, 1])
    coefficients = jnp.stack([part for entry in gate for part in entry], 1)
    coefficients = jnp.broadcast_to(coefficients[:, :, None], (circuits, 8, 128))
    smem = pl.BlockSpec(memory_space=pltpu.SMEM)
    vmem = pl.BlockSpec(memory_space=pltpu.VMEM)
    groups = circuits // GROUP
    return pl.pallas_call(
        functools.partial(fused_kernel, layers, ens, amp),
        out_shape=jax.ShapeDtypeStruct((2, circuits, 128), jnp.float32),
        in_specs=[smem, smem, smem, vmem, vmem],
        out_specs=vmem,
        scratch_shapes=layers_scratch(rows)
        + [
            pltpu.VMEM((circuits, rows, 2 * ORDER), jnp.bfloat16),
            pltpu.VMEM((2, total, share, 2 * ORDER), jnp.bfloat16),
            pltpu.VMEM((total, 8, 128), jnp.float32),
            pltpu.VMEM((total, 16, depth), jnp.bfloat16),
            pltpu.VMEM((2 * ens * GROUP, 16, depth), jnp.bfloat16),
            pltpu.VMEM((2, 128, 128), jnp.float32),
            pltpu.VMEM((2, total, 128), jnp.float32),
            pltpu.VMEM((ens * amp - 1, 2, circuits, 128), jnp.float32),
            pltpu.SemaphoreType.DMA((groups, 2 * ens - 1)),
            pltpu.SemaphoreType.DMA((groups, 2 * ens - 1)),
            pltpu.SemaphoreType.DMA((ens - 1,)),
            pltpu.SemaphoreType.DMA((ens - 1,)),
            pltpu.SemaphoreType.DMA((ens * amp - 1,)),
            pltpu.SemaphoreType.DMA((ens * amp - 1,)),
        ],
        compiler_params=pltpu.CompilerParams(
            vmem_limit_bytes=48 << 20, collective_id=0, has_side_effects=True
        ),
    )(*small_tables(layer_angles, entangler), coefficients, states)


def finish(summed, states, circuits):
    columns = lax.axis_size("ens") * circuits // lax.axis_size("amp")
    row_index = lax.axis_index("ens") * circuits + jnp.arange(circuits, dtype=jnp.int32)
    column_index = lax.axis_index("amp") * columns + jnp.arange(columns, dtype=jnp.int32)
    off_diagonal = jnp.where(row_index[:, None] == column_index[None, :], 0.0, 1.0).astype(jnp.float32)
    amplitudes = states.shape[2] * lax.axis_size("amp")
    return summed * (off_diagonal / math.sqrt(amplitudes))[None]


def fits(states):
    circuits, _, local = states.shape
    ens = lax.axis_size("ens")
    rows = local // ORDER
    return (
        rows % (2 * ens * 16) == 0 and circuits % 8 == 0 and ens * circuits % 16 == 0
        and ens * circuits <= 128 and lax.axis_size("amp") >= 2 and local <= 1 << 16 and ens > 1
    )


def scaled(coefficient, amplitudes):
    real_c = coefficient[0][:, None]
    imag_c = coefficient[1][:, None]
    return jnp.stack(
        [
            real_c * amplitudes[:, 0] - imag_c * amplitudes[:, 1],
            real_c * amplitudes[:, 1] + imag_c * amplitudes[:, 0],
        ],
        1,
    )


def choose_pair(upper_side, when_lower, when_upper):
    return (
        jnp.where(upper_side == 0, when_lower[0], when_upper[0]),
        jnp.where(upper_side == 0, when_lower[1], when_upper[1]),
    )


def pair_tile(mine, remote):
    products = jnp.einsum("ipa,jqa->pqij", mine, remote, preferred_element_type=jnp.float32)
    return jnp.stack([products[0, 0] + products[1, 1], products[0, 1] - products[1, 0]])


def body(states, layer_angles, entangler, global_angles):
    circuits = states.shape[0]
    if fits(states):
        summed = fused(states, layer_angles, entangler, global_angles)
        columns = lax.axis_size("ens") * circuits // lax.axis_size("amp")
        summed = lax.dynamic_slice_in_dim(summed, lax.axis_index("amp") * columns, columns, 2)
        return finish(summed, states, circuits)
    turned = all_layers(states, layer_angles, entangler).reshape(circuits, -1, 2, ORDER)
    current = jnp.swapaxes(turned, 1, 2).reshape(states.shape)
    swap_bit = lax.axis_size("amp").bit_length() - 2
    upper_side = lax.axis_index("amp") // 2**swap_bit % 2
    gate = rotation(global_angles[:, 0], global_angles[:, 1])
    partner = from_partner(current, "amp", swap_bit)
    coeff_self = choose_pair(upper_side, gate[0], gate[3])
    coeff_other = choose_pair(upper_side, gate[1], gate[2])
    final_states = (
        scaled(coeff_self, current.astype(jnp.float32))
        + scaled(coeff_other, partner.astype(jnp.float32))
    ).astype(jnp.bfloat16)
    partials = pair_tile(final_states, lax.all_gather(final_states, "ens", axis=0, tiled=True))
    summed = lax.psum_scatter(partials, "amp", scatter_dimension=2, tiled=True)
    return finish(summed, states, circuits)


def solution(mesh):
    return jax.shard_map(
        body,
        mesh=mesh,
        in_specs=(
            P(("groups", "ens"), None, "amp"),
            P(("groups", "ens"), None, None, None),
            P(("groups", "ens"), None, None),
            P(("groups", "ens"), None),
        ),
        out_specs=P(None, ("groups", "ens"), "amp"),
        check_vma=False,
    )
```

```python
import functools
import math

import jax
import jax.numpy as jnp
from jax import lax
from jax.experimental import pallas as pl
from jax.experimental.pallas import tpu as pltpu
from jax.sharding import PartitionSpec as P

JOINED = 7
TABLE = 64
ORDER = 2**JOINED
LOW = 3
GROUP = 1


def from_partner(array, axis, bit):
    return lax.ppermute(array, axis, [(i, i ^ 1 << bit) for i in range(lax.axis_size(axis))])


def rotation(polar_index, azimuth_index):
    polar = polar_index.astype(jnp.float32) * (math.pi / TABLE)
    azimuth = azimuth_index.astype(jnp.float32) * (math.pi / TABLE)
    cos_polar = jnp.cos(polar)
    sin_polar = jnp.sin(polar)
    cos_azim = jnp.cos(azimuth)
    sin_azim = jnp.sin(azimuth)
    return (
        (cos_azim * cos_polar, -sin_azim * cos_polar),
        (-cos_azim * sin_polar, sin_azim * sin_polar),
        (cos_azim * sin_polar, sin_azim * sin_polar),
        (cos_azim * cos_polar, sin_azim * cos_polar),
    )


def bit_of(shape, dim, bit, shift=0):
    return (lax.broadcasted_iota(jnp.int32, shape, dim) >> (bit - shift)) & 1


def part_factor(cos_ref, sin_ref, flip_ref, at, upper, high):
    qubits = range(LOW, JOINED) if high else range(LOW)
    shape = (2 ** len(qubits), ORDER)
    shift = LOW if high else 0
    row = {k: bit_of(shape, 0, k, shift) for k in qubits}
    lane = {k: bit_of(shape, 1, k) for k in range(JOINED)}
    out = row if upper else lane
    real = imag = None
    turn = None
    for k in qubits:
        cos_t, sin_t = cos_ref[at * 14 + 2 * k], sin_ref[at * 14 + 2 * k]
        cos_f, sin_f = cos_ref[at * 14 + 2 * k + 1], sin_ref[at * 14 + 2 * k + 1]
        side = (2 * out[k] - 1).astype(jnp.float32)
        factor = jnp.where(row[k] == lane[k], cos_t, side * sin_t)
        turn = factor if turn is None else turn * factor
        step = side * sin_f
        if real is None:
            real, imag = jnp.full(shape, cos_f), step
        else:
            real, imag = real * cos_f - imag * step, real * step + imag * cos_f
    for k in range(JOINED - 1):
        inside = k in qubits and k + 1 in qubits
        if inside or (not upper and not high and k == LOW - 1):
            turn = jnp.where(out[k] * out[k + 1] == 1, flip_ref[at * 6 + k] * turn, turn)
    return real * turn, imag * turn


def build(cos_ref, sin_ref, flip_ref, at, upper, w_ref):
    low_real, low_imag = part_factor(cos_ref, sin_ref, flip_ref, at, upper, False)
    high_real, high_imag = part_factor(cos_ref, sin_ref, flip_ref, at, upper, True)
    lows = [(low_real, low_imag)] * 2
    if upper:
        crossed = bit_of(low_real.shape, 0, LOW - 1) == 1
        flip = flip_ref[at * 6 + LOW - 1]
        lows[1] = tuple(jnp.where(crossed, flip * v, v) for v in lows[0])
    for pair in range(ORDER // 16):
        reals, imags = [], []
        for odd in range(2):
            r = 2 * pair + odd
            a_real = jnp.broadcast_to(high_real[r : r + 1], (8, ORDER))
            a_imag = jnp.broadcast_to(high_imag[r : r + 1], (8, ORDER))
            b_real, b_imag = lows[odd]
            reals.append(a_real * b_real - a_imag * b_imag)
            imags.append(a_real * b_imag + a_imag * b_real)
        real = jnp.concatenate(reals, 0)
        imag = jnp.concatenate(imags, 0)
        plus, minus = imag.astype(jnp.bfloat16), (-imag).astype(jnp.bfloat16)
        real = real.astype(jnp.bfloat16)
        top, bottom = (minus, plus) if upper else (plus, minus)
        rows = pl.ds(16 * pair, 16)
        rows_below = pl.ds(ORDER + 16 * pair, 16)
        w_ref[rows, :ORDER] = real
        w_ref[rows, ORDER:] = top
        w_ref[rows_below, :ORDER] = bottom
        w_ref[rows_below, ORDER:] = real


def bridge(values):
    rows, columns = values.shape
    shape = (1, 8, columns)
    odd = bit_of(shape, 1, 0) * bit_of(shape, 2, JOINED - 1)
    sign = (1 - 2 * odd).astype(jnp.float32)
    return (values.reshape(rows // 8, 8, columns) * sign).reshape(rows, columns)


def run_layers(first, layers, cos_ref, sin_ref, flip_ref, x_refs, t_refs, wl_ref, wu_ref, s_ref):
    rows = t_refs[0].shape[0]
    blocks = rows // ORDER
    many = len(t_refs)
    for i in range(many):

        def spread(step, carry, i=i):
            flat = x_refs[i][:, pl.ds(pl.multiple_of(step * 16 * ORDER, 16 * ORDER), 16 * ORDER)]
            tiles = flat.astype(jnp.float32).reshape(2, 16, ORDER).astype(jnp.bfloat16)
            rows_at = pl.ds(pl.multiple_of(step * 16, 16), 16)
            t_refs[i][rows_at, :ORDER] = tiles[0]
            t_refs[i][rows_at, ORDER:] = tiles[1]
            return carry

        lax.fori_loop(0, rows // 16, spread, 0, unroll=4)
        build(cos_ref, sin_ref, flip_ref, (first + i) * layers, False, wl_ref.at[i])

    def two(pair, carry):
        layer = 2 * pair
        following = jnp.minimum(layer + 2, layers - 2)
        for i in range(many):
            at = (first + i) * layers
            y = jnp.dot(t_refs[i][...], wl_ref[i], preferred_element_type=jnp.float32)
            y = bridge(y).astype(jnp.bfloat16)
            for b in range(blocks):
                for p in range(2):
                    s_ref[i, p * ORDER : (p + 1) * ORDER, b * ORDER : (b + 1) * ORDER] = y[
                        b * ORDER : (b + 1) * ORDER, p * ORDER : (p + 1) * ORDER
                    ]
            build(cos_ref, sin_ref, flip_ref, at + layer + 1, True, wu_ref.at[i])
        for i in range(many):
            at = (first + i) * layers
            y = jnp.dot(wu_ref[i], s_ref[i], preferred_element_type=jnp.float32)
            y = bridge(y).astype(jnp.bfloat16)
            for b in range(blocks):
                for p in range(2):
                    t_refs[i][b * ORDER : (b + 1) * ORDER, p * ORDER : (p + 1) * ORDER] = y[
                        p * ORDER : (p + 1) * ORDER, b * ORDER : (b + 1) * ORDER
                    ]
            build(cos_ref, sin_ref, flip_ref, at + following, False, wl_ref.at[i])
        return carry

    lax.fori_loop(0, layers // 2, two, 0)


def layers_scratch(rows):
    return [
        pltpu.VMEM((GROUP, 2 * ORDER, 2 * ORDER), jnp.bfloat16),
        pltpu.VMEM((GROUP, 2 * ORDER, 2 * ORDER), jnp.bfloat16),
        pltpu.VMEM((GROUP, 2 * ORDER, rows), jnp.bfloat16),
    ]


def layers_kernel(layers, cos_ref, sin_ref, flip_ref, x_ref, t_ref, wl_ref, wu_ref, s_ref):
    first = pl.program_id(0) * GROUP
    run_layers(
        first, layers, cos_ref, sin_ref, flip_ref,
        [x_ref.at[i] for i in range(GROUP)], [t_ref.at[i] for i in range(GROUP)],
        wl_ref, wu_ref, s_ref,
    )


def small_tables(layer_angles, entangler):
    angle = layer_angles.astype(jnp.float32).reshape(-1) * (math.pi / TABLE)
    flip = 1.0 - 2.0 * entangler.astype(jnp.float32).reshape(-1)
    return jnp.cos(angle), jnp.sin(angle), flip


def all_layers(states, layer_angles, entangler):
    circuits, _, local = states.shape
    rows = local // ORDER
    layers = layer_angles.shape[1]
    smem = pl.BlockSpec(memory_space=pltpu.SMEM)
    return pl.pallas_call(
        functools.partial(layers_kernel, layers),
        grid=(circuits // GROUP,),
        out_shape=jax.ShapeDtypeStruct((circuits, rows, 2 * ORDER), jnp.bfloat16),
        in_specs=[smem, smem, smem, pl.BlockSpec((GROUP, 2, local), lambda g: (g, 0, 0))],
        out_specs=pl.BlockSpec((GROUP, rows, 2 * ORDER), lambda g: (g, 0, 0)),
        scratch_shapes=layers_scratch(rows),
        compiler_params=pltpu.CompilerParams(vmem_limit_bytes=32 << 20),
    )(*small_tables(layer_angles, entangler), states)


MESH_ID = pl.DeviceIdType.MESH


def gate_pair(gate, low, high):
    outs = []
    for r in range(2):
        a_real, a_imag, b_real, b_imag = (gate[4 * r + k : 4 * r + k + 1] for k in range(4))
        real = a_real * low[0] - a_imag * low[1] + (b_real * high[0] - b_imag * high[1])
        imag = a_real * low[1] + a_imag * low[0] + (b_real * high[1] + b_imag * high[0])
        outs.append((real, imag))
    return outs


def fused_kernel(
    layers, ens, amp,
    cos_ref, sin_ref, flip_ref, gate_ref, x_ref, o_ref,
    wl_ref, wu_ref, s_ref, t_ref, r_ref, c_ref, f_ref, h_ref, l_ref, p_ref, q_ref,
    send_sem, recv_sem, gate_send, gate_recv, sum_send, sum_recv,
):
    circuits, rows, _ = t_ref.shape
    groups = circuits // GROUP
    share = rows // (2 * ens)
    parts = share // 16
    bit = amp.bit_length() - 2
    me = lax.axis_index("ens")
    here = lax.axis_index("amp")
    side = (here // 2**bit) % 2
    rest = here - side * 2**bit

    barrier = pltpu.get_barrier_semaphore()
    everyone = [(k // amp, k % amp) for k in range(1, ens * amp)]
    for e, a in everyone:
        pl.semaphore_signal(
            barrier, inc=1, device_id={"ens": (me + e) % ens, "amp": (here + a) % amp}, device_id_type=MESH_ID
        )
    pl.semaphore_wait(barrier, len(everyone))

    def gate_copy(k, source):
        return pltpu.make_async_remote_copy(
            src_ref=gate_ref,
            dst_ref=c_ref.at[pl.ds(source * circuits, circuits)],
            send_sem=gate_send.at[k - 1],
            recv_sem=gate_recv.at[k - 1],
            device_id={"ens": (me + k) % ens},
            device_id_type=MESH_ID,
        )

    for k in range(1, ens):
        gate_copy(k, me).start()
    c_ref[pl.ds(me * circuits, circuits)] = gate_ref[...]

    peers = sorted(((k // ens, k % ens) for k in range(1, 2 * ens)), key=lambda p: (abs(2 * p[1] - ens), p[0]))

    def piece(k, group, from_side, from_ens):
        across, along = peers[k]
        to_side = side + across - 2 * side * across
        to_ens = (me + along) % ens
        start = pl.multiple_of((to_side * ens + to_ens) * share, share)
        return pltpu.make_async_remote_copy(
            src_ref=t_ref.at[pl.ds(group * GROUP, GROUP), pl.ds(start, share)],
            dst_ref=r_ref.at[from_side, pl.ds(from_ens * circuits + group * GROUP, GROUP)],
            send_sem=send_sem.at[group, k],
            recv_sem=recv_sem.at[group, k],
            device_id={"ens": to_ens, "amp": to_side * 2**bit + rest},
            device_id_type=MESH_ID,
        )

    def compute(group, carry):
        first = group * GROUP
        run_layers(
            first, layers, cos_ref, sin_ref, flip_ref,
            [x_ref.at[first + i] for i in range(GROUP)], [t_ref.at[first + i] for i in range(GROUP)],
            wl_ref, wu_ref, s_ref,
        )
        for k in range(len(peers)):
            piece(k, group, side, me).start()
        own = pl.multiple_of((side * ens + me) * share, share)
        for i in range(GROUP):
            r_ref[side, me * circuits + first + i] = t_ref[first + i, pl.ds(own, share), :]
        return carry

    lax.fori_loop(0, groups, compute, 0)
    for k in range(1, ens):
        gate_copy(k, (me + ens - k) % ens).wait_recv()

    total = ens * circuits
    fresh = ens * GROUP
    depth = f_ref.shape[2]
    l_ref[...] = jnp.zeros_like(l_ref)

    for group in range(groups):
        for k, (across, along) in enumerate(peers):
            piece(k, group, side + across - 2 * side * across, (me + ens - along) % ens).wait_recv()

        def one(step, inner, group=group):
            which = (step // GROUP) * circuits + group * GROUP + step % GROUP
            gate = c_ref[which]
            low = r_ref[0, which].astype(jnp.float32)
            high = r_ref[1, which].astype(jnp.float32)
            outs = gate_pair(gate, (low[:, :ORDER], low[:, ORDER:]), (high[:, :ORDER], high[:, ORDER:]))
            for x, (real, imag) in enumerate(outs):
                real = real.astype(jnp.bfloat16)
                minus = (-real).astype(jnp.bfloat16)
                imag = imag.astype(jnp.bfloat16)
                for part in range(parts):
                    at = (x * parts + part) * 2 * ORDER
                    take = slice(16 * part, 16 * part + 16)
                    for ref, row in ((f_ref, group * fresh + step), (h_ref, step)):
                        ref[row, :, at : at + ORDER] = real[take]
                        ref[row, :, at + ORDER : at + 2 * ORDER] = imag[take]
                    h_ref[fresh + step, :, at : at + ORDER] = imag[take]
                    h_ref[fresh + step, :, at + ORDER : at + 2 * ORDER] = minus[take]
            return inner

        lax.fori_loop(0, fresh, one, 0)
        known = (group + 1) * fresh
        lhs = f_ref[:known].reshape(known * 16, depth)
        rhs = h_ref[...].reshape(2 * fresh * 16, depth)
        full = lax.dot_general(lhs, rhs, (((1,), (1,)), ((), ())), preferred_element_type=jnp.float32)
        shape = (1, 16, 2 * fresh * 16)
        same = lax.broadcasted_iota(jnp.int32, shape, 1) == lax.broadcasted_iota(jnp.int32, shape, 2) % 16
        kept = jnp.where(same, full.reshape(known, 16, 2 * fresh * 16), 0.0).sum(1)
        pick_shape = (fresh * 16, 128)
        pick = lax.broadcasted_iota(jnp.int32, pick_shape, 0) // 16 + group * fresh
        pick = (pick == lax.broadcasted_iota(jnp.int32, pick_shape, 1)).astype(jnp.float32)
        for which in range(2):
            l_ref[which, :known] += jnp.dot(
                kept[:, which * fresh * 16 : (which + 1) * fresh * 16], pick,
                precision=lax.Precision.HIGHEST, preferred_element_type=jnp.float32,
            )

    square = (128, 128)
    row = lax.broadcasted_iota(jnp.int32, square, 0)
    column = lax.broadcasted_iota(jnp.int32, square, 1)
    place = (row % circuits // GROUP) * fresh + row // circuits * GROUP + row % GROUP
    order = jnp.where((place == column) & (row < total), 1.0, 0.0)
    for which in range(2):
        half = l_ref[which]
        above = jnp.where(row // fresh < column // fresh, half, 0.0)
        mirrored = jnp.transpose(above)
        whole = half + mirrored if which == 0 else half - mirrored
        moved = jnp.dot(order, whole, precision=lax.Precision.HIGHEST, preferred_element_type=jnp.float32)
        p_ref[which] = lax.dot_general(
            moved, order, (((1,), (1,)), ((), ())),
            precision=lax.Precision.HIGHEST, preferred_element_type=jnp.float32,
        )[:total]

    def slab(k):
        e, a = everyone[k]
        to = (me + e) % ens
        return pltpu.make_async_remote_copy(
            src_ref=p_ref.at[:, pl.ds(pl.multiple_of(to * circuits, circuits), circuits)],
            dst_ref=q_ref.at[k],
            send_sem=sum_send.at[k],
            recv_sem=sum_recv.at[k],
            device_id={"ens": to, "amp": (here + a) % amp},
            device_id_type=MESH_ID,
        )

    for k in range(len(everyone)):
        slab(k).start()
    result = p_ref[:, pl.ds(pl.multiple_of(me * circuits, circuits), circuits), :]
    for k in range(len(everyone)):
        slab(k).wait_recv()
        result = result + q_ref[k]
    o_ref[...] = result
    for k in range(len(everyone)):
        slab(k).wait_send()
    for k in range(1, ens):
        gate_copy(k, me).wait_send()

    def drain(group, carry):
        for k in range(len(peers)):
            piece(k, group, side, me).wait_send()
        return carry

    lax.fori_loop(0, groups, drain, 0)


def fused(states, layer_angles, entangler, global_angles):
    circuits, _, local = states.shape
    rows = local // ORDER
    layers = layer_angles.shape[1]
    ens, amp = lax.axis_size("ens"), lax.axis_size("amp")
    total = ens * circuits
    share = rows // (2 * ens)
    depth = 2 * (share // 16) * 2 * ORDER
    gate = rotation(global_angles[:, 0], global_angles[:, 1])
    coefficients = jnp.stack([part for entry in gate for part in entry], 1)
    coefficients = jnp.broadcast_to(coefficients[:, :, None], (circuits, 8, 128))
    smem = pl.BlockSpec(memory_space=pltpu.SMEM)
    vmem = pl.BlockSpec(memory_space=pltpu.VMEM)
    groups = circuits // GROUP
    return pl.pallas_call(
        functools.partial(fused_kernel, layers, ens, amp),
        out_shape=jax.ShapeDtypeStruct((2, circuits, 128), jnp.float32),
        in_specs=[smem, smem, smem, vmem, vmem],
        out_specs=vmem,
        scratch_shapes=layers_scratch(rows)
        + [
            pltpu.VMEM((circuits, rows, 2 * ORDER), jnp.bfloat16),
            pltpu.VMEM((2, total, share, 2 * ORDER), jnp.bfloat16),
            pltpu.VMEM((total, 8, 128), jnp.float32),
            pltpu.VMEM((total, 16, depth), jnp.bfloat16),
            pltpu.VMEM((2 * ens * GROUP, 16, depth), jnp.bfloat16),
            pltpu.VMEM((2, 128, 128), jnp.float32),
            pltpu.VMEM((2, total, 128), jnp.float32),
            pltpu.VMEM((ens * amp - 1, 2, circuits, 128), jnp.float32),
            pltpu.SemaphoreType.DMA((groups, 2 * ens - 1)),
            pltpu.SemaphoreType.DMA((groups, 2 * ens - 1)),
            pltpu.SemaphoreType.DMA((ens - 1,)),
            pltpu.SemaphoreType.DMA((ens - 1,)),
            pltpu.SemaphoreType.DMA((ens * amp - 1,)),
            pltpu.SemaphoreType.DMA((ens * amp - 1,)),
        ],
        compiler_params=pltpu.CompilerParams(
            vmem_limit_bytes=48 << 20, collective_id=0, has_side_effects=True
        ),
    )(*small_tables(layer_angles, entangler), coefficients, states)


def finish(summed, states, circuits):
    columns = lax.axis_size("ens") * circuits // lax.axis_size("amp")
    row_index = lax.axis_index("ens") * circuits + jnp.arange(circuits, dtype=jnp.int32)
    column_index = lax.axis_index("amp") * columns + jnp.arange(columns, dtype=jnp.int32)
    off_diagonal = jnp.where(row_index[:, None] == column_index[None, :], 0.0, 1.0).astype(jnp.float32)
    amplitudes = states.shape[2] * lax.axis_size("amp")
    return summed * (off_diagonal / math.sqrt(amplitudes))[None]


def fits(states):
    circuits, _, local = states.shape
    ens = lax.axis_size("ens")
    rows = local // ORDER
    return (
        rows % (2 * ens * 16) == 0 and circuits % 8 == 0 and ens * circuits % 16 == 0
        and ens * circuits <= 128 and lax.axis_size("amp") >= 2 and local <= 1 << 16 and ens > 1
    )


def scaled(coefficient, amplitudes):
    real_c = coefficient[0][:, None]
    imag_c = coefficient[1][:, None]
    return jnp.stack(
        [
            real_c * amplitudes[:, 0] - imag_c * amplitudes[:, 1],
            real_c * amplitudes[:, 1] + imag_c * amplitudes[:, 0],
        ],
        1,
    )


def choose_pair(upper_side, when_lower, when_upper):
    return (
        jnp.where(upper_side == 0, when_lower[0], when_upper[0]),
        jnp.where(upper_side == 0, when_lower[1], when_upper[1]),
    )


def pair_tile(mine, remote):
    products = jnp.einsum("ipa,jqa->pqij", mine, remote, preferred_element_type=jnp.float32)
    return jnp.stack([products[0, 0] + products[1, 1], products[0, 1] - products[1, 0]])


def body(states, layer_angles, entangler, global_angles):
    circuits = states.shape[0]
    if fits(states):
        summed = fused(states, layer_angles, entangler, global_angles)
        columns = lax.axis_size("ens") * circuits // lax.axis_size("amp")
        summed = lax.dynamic_slice_in_dim(summed, lax.axis_index("amp") * columns, columns, 2)
        return finish(summed, states, circuits)
    turned = all_layers(states, layer_angles, entangler).reshape(circuits, -1, 2, ORDER)
    current = jnp.swapaxes(turned, 1, 2).reshape(states.shape)
    swap_bit = lax.axis_size("amp").bit_length() - 2
    upper_side = lax.axis_index("amp") // 2**swap_bit % 2
    gate = rotation(global_angles[:, 0], global_angles[:, 1])
    partner = from_partner(current, "amp", swap_bit)
    coeff_self = choose_pair(upper_side, gate[0], gate[3])
    coeff_other = choose_pair(upper_side, gate[1], gate[2])
    final_states = (
        scaled(coeff_self, current.astype(jnp.float32))
        + scaled(coeff_other, partner.astype(jnp.float32))
    ).astype(jnp.bfloat16)
    partials = pair_tile(final_states, lax.all_gather(final_states, "ens", axis=0, tiled=True))
    summed = lax.psum_scatter(partials, "amp", scatter_dimension=2, tiled=True)
    return finish(summed, states, circuits)


def solution(mesh):
    return jax.shard_map(
        body,
        mesh=mesh,
        in_specs=(
            P(("groups", "ens"), None, "amp"),
            P(("groups", "ens"), None, None, None),
            P(("groups", "ens"), None, None),
            P(("groups", "ens"), None),
        ),
        out_specs=P(None, ("groups", "ens"), "amp"),
        check_vma=False,
    )
```
